256 devices in a mesh: seq: 32 (over y, z), expert: 8 (over x, core).
Axes of the slice: x: 4, y: 4, z: 8, core: 2. Of those that a mesh axis runs over, the one named last changes fastest.
Arguments:
- residual: bfloat16 [16384, 2304], P(('seq', 'expert')), may hold values from -6 to 6
- query_rows: bfloat16 [16384, 4096], P('seq', 'expert'), may hold values from -6 to 6
- key_rows: bfloat16 [16384, 4096], P('seq', 'expert'), may hold values from -6 to 6
- value_rows: bfloat16 [16384, 4096], P('seq', 'expert'), may hold values from -6 to 6
- log_decay: float32 [16384, 4096], P('seq', 'expert'), may hold values from -0.7 to 0
- write_rate: float32 [16384, 32], P('seq', 'expert'), may hold values from 0 to 1
- output_weight: bfloat16 [4096, 2304], P('expert'), may hold values from -0.09375 to 0.09375
- routes: int32 [16384, 8], P(('seq', 'expert')), may hold values from 0 to 255, all different within a row; in each aligned block of 64 rows (0 to 63, 64 to 127, ...) at most 4 rows name the same one
- route_gates: float32 [16384, 8], P(('seq', 'expert')), may hold values from 0.1 to 0.6
- expert_up: bfloat16 [256, 2304, 1024], P(('seq', 'expert')), may hold values from -0.125 to 0.125
- expert_down: bfloat16 [256, 512, 2304], P(('seq', 'expert')), may hold values from -0.25 to 0.25
Outputs:
- layer_out: bfloat16 [16384, 2304], P(('seq', 'expert'))
The draws below stay inside these ranges and needn't reach their ends.
Inputs may be any that keep to these rules, and one draw needn't show every extreme that they name: `routes`: each row names 8 different experts. In each aligned block of 64 rows no expert is named by more than 4 rows, and in some block one expert is named by exactly 4.
All inputs are finite; a program needn't handle non-finite values.
Results may differ from the reference program's by a relative error of at most 0.007.
Values may be sent and summed in bfloat16 or wider, within the bound.
No kernel may reach another device: no remote copies, remote signals or barrier semaphores. Data moves between devices by JAX's collectives and lax.ppermute only.
A program may use at most 128 MiB of HBM per device.

```python
import math
import jax
import jax.numpy as jnp
import numpy as np
from jax import lax

D = 2304
HEADS = 32
DK = 128
FFW = 512
TOP = 8
TOKENS = 16384
ROWS = 64
EXPERTS = 256
CAP = 4


def head_speed(key):
    chance = jax.random.uniform(jax.random.fold_in(key, 11), (HEADS,), jnp.float32)
    limit = 0.5
    return jnp.where(chance < limit, 1.0, 0.0).astype(jnp.float32)


def spread_log(key, shape, low, high):
    return jnp.exp(jax.random.uniform(key, shape, jnp.float32, math.log(low), math.log(high)))


def draw_key_rows(key, part):
    direction = jax.random.normal(jax.random.fold_in(key, 41), (1, HEADS, DK), jnp.float32)
    noise_part = jax.random.normal(jax.random.fold_in(key, 42), (TOKENS, HEADS, DK), jnp.float32)
    combined = jnp.clip(2.5 * direction + noise_part, -6.0, 6.0)
    return combined.reshape(TOKENS, HEADS * DK).astype(jnp.bfloat16)


def draw_log_decay(key, part):
    slow = head_speed(key)[:, None]
    fast_rate = spread_log(jax.random.fold_in(key, 21), (HEADS, DK), 1.0 / 60.0, 1.0 / 20.0)
    slow_rate = spread_log(jax.random.fold_in(key, 22), (HEADS, DK), 0.05 / TOKENS, 0.5 / TOKENS)
    write_strength = slow * slow_rate + (1.0 - slow) * fast_rate
    random_noise = spread_log(jax.random.fold_in(key, 23), (TOKENS, HEADS, DK), 0.5, 2.0)
    leading_slot_rank = jax.random.randint(jax.random.fold_in(key, 24), (HEADS,), 0, TOKENS)
    step_apart = jax.random.randint(jax.random.fold_in(key, 26), (HEADS,), 1, TOKENS)
    runner_slot_rank = (leading_slot_rank + step_apart) % TOKENS
    retained_entries = jax.random.uniform(jax.random.fold_in(key, 25), (2, HEADS), jnp.float32, 0.55, 0.8)
    slot_ranks = jnp.arange(TOKENS)[:, None]
    spike_amount = jnp.where(slot_ranks == leading_slot_rank[None, :], jnp.log(retained_entries[0])[None, :], 0.0)
    spike_amount = spike_amount + jnp.where(slot_ranks == runner_slot_rank[None, :], jnp.log(retained_entries[1])[None, :], 0.0)
    routed_output = -write_strength[None, :, :] * random_noise + spike_amount[:, :, None]
    return routed_output.reshape(TOKENS, HEADS * DK).astype(jnp.float32)


def draw_write_rate(key, part):
    slow = head_speed(key)[None, :]
    fast = jax.random.uniform(jax.random.fold_in(key, 31), (TOKENS, HEADS), jnp.float32, 0.2, 0.9)
    slow_part = 0.3 * DK / TOKENS * spread_log(jax.random.fold_in(key, 32), (TOKENS, HEADS), 0.5, 2.0)
    return (slow * slow_part + (1.0 - slow) * fast).astype(jnp.float32)


def level_of(rng, dims, cuts, least, top_value):
    level, own = 1.0, jax.random.fold_in(rng, 6)
    for dim, shards_of in cuts:
        draws = jnp.exp(jax.random.uniform(jax.random.fold_in(own, dim), (shards_of,), jnp.float32, least / len(cuts), top_value / len(cuts)))
        level = level * jnp.repeat(draws, dims[dim] // shards_of).reshape([-1 if axis == dim else 1 for axis in range(len(dims))])
    return level


def assign_block(rng, own, number, rows, amount, top, most, skew):
    order = jax.random.permutation(rng, amount)
    crowded, ordinary = portions_of(amount, rows * top, most, skew, True), portions_of(amount, rows * top, most, skew, False)
    places = jnp.arange(amount)

    def named(tallies, turn):
        used = int((tallies > 0).sum())
        fixed = max(1, used // 4)
        passed = fixed + (places - fixed + turn * (used - fixed)) % max(1, amount - fixed)
        return jnp.zeros((amount,), jnp.int32).at[order[jnp.where(places < fixed, places, passed)]].set(jnp.asarray(tallies, jnp.int32))

    tallies = jnp.where(number % 4 == 0, named(crowded, number // 4), named(ordinary, number - number // 4 - 1))
    mixed = jax.random.permutation(jax.random.fold_in(own, 3), amount)
    donor, taker = mixed[0:amount // 2 * 2:2], mixed[1:amount // 2 * 2:2]
    room = jnp.minimum(tallies[donor] - 1, most - tallies[taker]) // 2
    room = jnp.where((donor == order[0]) | (taker == order[0]) | (tallies[taker] == 0), 0, jnp.maximum(room, 0))
    passed = jax.random.randint(jax.random.fold_in(own, 4), (amount // 2,), 0, 1 << 20) % (room + 1)
    tallies = tallies.at[donor].add(-passed).at[taker].add(passed)
    items = jnp.searchsorted(jnp.cumsum(tallies), jnp.arange(rows * top), side="right").astype(jnp.int32)
    table = items.reshape(top, rows).T
    table = table[jax.random.permutation(jax.random.fold_in(own, 1), rows)]
    turn = jax.random.randint(jax.random.fold_in(own, 2), (rows, 1), 0, top)
    return jnp.take_along_axis(table, (jnp.arange(top)[None, :] + turn) % top, axis=1)


def portions_of(number_of, total, most, lean, full):
    weights = [(1 << 20) // math.isqrt(rank ** lean) + 1 for rank in range(1, number_of + 1)]
    largest = most if full else min(most, max(-(-total // number_of), total * weights[0] // sum(weights)))
    least = 1 if total - largest >= number_of - 1 else 0
    holding, surplus = [largest] + [least] * (number_of - 1), total - largest - least * (number_of - 1)
    while surplus > 0:
        movable = [i for i in range(1, number_of) if holding[i] < largest] or [i for i in range(1, number_of) if holding[i] < most]
        whole, budget = sum([weights[i] for i in movable]), surplus
        for i in movable:
            more = min(most - holding[i], max(1, budget * weights[i] // whole), surplus)
            holding[i] = holding[i] + more
            surplus = surplus - more
    return np.array(holding)


def scatter_about(rng, extent, deviation, most, split=(), held_as=jnp.bfloat16):
    result = deviation * jax.random.normal(rng, extent, jnp.float32)
    if split:
        result = result * level_of(rng, extent, split, -0.22, 0.18)
    return jnp.clip(result, -most, most).astype(held_as)


def setup_inputs(seed: int = 0) -> dict:
    splits = jax.random.split(jax.random.key(seed), 12)
    residual = scatter_about(splits[0], (TOKENS, D), 1.0, 6.0, ((0, 256),))
    query_rows = scatter_about(splits[1], (TOKENS, HEADS * DK), 1.0, 6.0, ((0, 32), (1, 8)))
    key_rows = draw_key_rows(jax.random.fold_in(splits[11], 71), 0)
    value_rows = scatter_about(splits[3], (TOKENS, HEADS * DK), 1.0, 6.0, ((0, 32), (1, 8)))
    log_decay = draw_log_decay(jax.random.fold_in(splits[11], 71), 0)
    write_rate = draw_write_rate(jax.random.fold_in(splits[11], 71), 0)
    output_weight = scatter_about(splits[6], (HEADS * DK, D), (HEADS * DK) ** -0.5, 0.09375, ((0, 8),))
    routes_keys = jax.random.split(jax.random.fold_in(splits[7], 1), TOKENS // ROWS)
    routes_turns = jax.random.permutation(jax.random.fold_in(splits[7], 3), TOKENS // ROWS)
    routes = jax.vmap(lambda own, number: assign_block(jax.random.fold_in(splits[7], 2), own, number, ROWS, EXPERTS, TOP, CAP, 2))(routes_keys, routes_turns).reshape((TOKENS, TOP))
    route_gates = jnp.clip(0.1 + 0.5 * jax.random.uniform(splits[8], (TOKENS, TOP), jnp.float32) ** level_of(splits[8], (TOKENS, TOP), ((0, 256),), -0.2, 0.2), 0.1, 0.6)
    expert_up = scatter_about(splits[9], (EXPERTS, D, 2 * FFW), D ** -0.5, 0.125, ((0, 256),))
    expert_down = scatter_about(splits[10], (EXPERTS, FFW, D), FFW ** -0.5, 0.25, ((0, 256),))
    return dict(residual=residual, query_rows=query_rows, key_rows=key_rows, value_rows=value_rows, log_decay=log_decay, write_rate=write_rate, output_weight=output_weight, routes=routes, route_gates=route_gates, expert_up=expert_up, expert_down=expert_down)


def unit_rows(block):
    return block * lax.rsqrt(lax.optimization_barrier(jnp.sum(block * block, axis=-1, keepdims=True)) + 1e-06)

def reference(residual, query_rows, key_rows, value_rows, log_decay, write_rate, output_weight, routes, route_gates, expert_up, expert_down):
    precise = lax.Precision.HIGHEST
    queries = unit_rows(query_rows.astype(jnp.float32).reshape(TOKENS, HEADS, DK))
    keyed = unit_rows(key_rows.astype(jnp.float32).reshape(TOKENS, HEADS, DK))
    values = value_rows.astype(jnp.float32).reshape(TOKENS, HEADS, DK)
    decays = jnp.exp(log_decay.reshape(TOKENS, HEADS, DK))

    def advance(state, inputs):
        query_now, key_now, value_now, decay_now, rate_now = inputs
        state = state * decay_now[:, :, None]
        recalled = jnp.einsum('hd,hde->he', key_now, state, precision=precise)
        state = state + rate_now[:, None, None] * key_now[:, :, None] * (value_now - recalled)[:, None, :]
        return (state, jnp.einsum('hd,hde->he', query_now, state, precision=precise))
    initial = jnp.zeros((HEADS, DK, DK), jnp.float32)
    final_state, head_out = lax.scan(advance, initial, (queries, keyed, values, decays, write_rate))
    head_norm = head_out * lax.rsqrt(lax.optimization_barrier(jnp.mean(head_out * head_out, axis=-1, keepdims=True)) + 1e-06)
    head_norm = head_norm.astype(jnp.bfloat16).reshape(TOKENS, HEADS * DK)
    attended = jnp.dot(head_norm, output_weight, preferred_element_type=jnp.float32)
    mixed = (residual.astype(jnp.float32) + attended).astype(jnp.bfloat16)
    mixed_wide = mixed.astype(jnp.float32)
    expert_in = (mixed_wide * lax.rsqrt(lax.optimization_barrier(jnp.mean(mixed_wide * mixed_wide, axis=-1, keepdims=True)) + 1e-06)).astype(jnp.bfloat16)
    pair_expert = routes.reshape(-1).astype(jnp.int32)
    pair_token = (jnp.arange(TOKENS * TOP) // TOP).astype(jnp.int32)
    source = (pair_token // ROWS).astype(jnp.int32)
    sort_key = (source * EXPERTS + pair_expert).astype(jnp.int32)
    order = jnp.argsort(sort_key, stable=True).astype(jnp.int32)
    sorted_key = sort_key[order]
    leading_slot_rank = jnp.searchsorted(sorted_key, sorted_key, side='left').astype(jnp.int32)
    sorted_rank = (jnp.arange(TOKENS * TOP).astype(jnp.int32) - leading_slot_rank).astype(jnp.int32)
    rank = jnp.zeros((TOKENS * TOP,), jnp.int32).at[order].set(sorted_rank)
    slot = (source * CAP + rank).astype(jnp.int32)
    token_table = jnp.full((EXPERTS, EXPERTS * CAP), TOKENS, jnp.int32).at[pair_expert, slot].set(pair_token)
    gate_table = jnp.zeros((EXPERTS, EXPERTS * CAP), jnp.float32).at[pair_expert, slot].set(route_gates.reshape(-1).astype(jnp.float32))
    padded = jnp.concatenate([expert_in, jnp.zeros((1, D), jnp.bfloat16)], axis=0)

    def run_expert(total, inputs):
        token_ids, gate_values, weight_up, weight_down = inputs
        rows_in = padded[token_ids]
        gate_up = jnp.dot(rows_in, weight_up, preferred_element_type=jnp.float32)
        hidden = (jax.nn.silu(gate_up[:, :FFW]) * gate_up[:, FFW:]).astype(jnp.bfloat16)
        routed_output = jnp.dot(hidden, weight_down, preferred_element_type=jnp.float32).astype(jnp.bfloat16)
        total = total.at[token_ids].add(gate_values[:, None] * routed_output.astype(jnp.float32))
        return (total, None)
    start_total = jnp.zeros((TOKENS + 1, D), jnp.float32)
    total, unused = lax.scan(run_expert, start_total, (token_table, gate_table, expert_up, expert_down))
    return (mixed_wide + total[:TOKENS]).astype(jnp.bfloat16)
```

```python
import jax
import jax.numpy as jnp
from jax import lax
from jax.experimental import pallas as pl
from jax.experimental.pallas import tpu as pltpu
from jax.sharding import Mesh
from jax.sharding import PartitionSpec as P

CHUNK = 64
PER_STEP = 2
DK = 128
SLOTS = 32
Z, Y, X, C = "seq_1", "seq_0", "lane", "core"
ALL = (Y, Z, X, C)
PLANE = (Y, X, C)
BF = jnp.bfloat16
F32 = jnp.float32
INTERPRET = False


def split2(x):
    hi = x.astype(BF)
    return hi, (x - hi.astype(F32)).astype(BF)


def dg(a, b, dims):
    return lax.dot_general(a, b, (dims, ((), ())), preferred_element_type=F32)


NN = ((1,), (0,))
NT = ((1,), (1,))
TN = ((0,), (0,))


def dot3(a, b, dims=NN):
    ah, al = split2(a)
    bh, bl = split2(b)
    return dg(ah, bh, dims) + (dg(ah, bl, dims) + dg(al, bh, dims))


def exact_left(a, b, dims=NN):
    bh, bl = split2(b)
    return dg(a, bh, dims) + dg(a, bl, dims)


def unit_rows(x):
    return x * lax.rsqrt(jnp.sum(x * x, axis=-1, keepdims=True) + 1e-06)


def iota2(shape, dim):
    return lax.broadcasted_iota(jnp.int32, shape, dim)


def unit_lower_inverse(low):
    n = CHUNK
    row, col = iota2((n, n), 0), iota2((n, n), 1)
    eye = jnp.where(row == col, 1.0, 0.0)
    inner = jnp.where(row // 8 == col // 8, low, 0.0)
    second = dot3(inner, inner)
    fourth = dot3(second, second)
    inv = eye - inner
    inv = inv + dot3(inv, second)
    inv = inv + dot3(inv, fourth)
    size = 16
    while size <= n:
        half = size // 2
        between = (row // size == col // size) & (row // half != col // half)
        cross = jnp.where(between, low, 0.0)
        inv = inv - dot3(inv, dot3(cross, inv))
        size *= 2
    return inv


def local_kernel(q_ref, k_ref, v_ref, ld_ref, wr_ref, ext_ref, pair_ref, state_ref):
    step = pl.program_id(0)
    heads = wr_ref.shape[1]
    n = CHUNK

    @pl.when(step == 0)
    def _():
        eye = jnp.where(iota2((DK, DK), 0) == iota2((DK, DK), 1), 1.0, 0.0)
        start = jnp.concatenate([eye, jnp.zeros((DK, DK), F32)], axis=1)
        for h in range(heads):
            state_ref[h] = start

    row, col = iota2((n, n), 0), iota2((n, n), 1)
    strict, causal = row > col, row >= col
    tri = jnp.where(causal, 1.0, 0.0).astype(BF)
    eye128 = iota2((DK, DK), 0) == iota2((DK, DK), 1)
    prepared = []
    for c in range(PER_STEP):
        rows = slice(c * n, (c + 1) * n)
        logs = ld_ref[rows, :]
        one, rest = logs.astype(BF), logs
        rest = logs - one.astype(F32)
        two, three = split2(rest)
        summed_all = dg(tri, one, NN) + (dg(tri, two, NN) + dg(tri, three, NN))
        for h in range(heads):
            lanes = slice(h * DK, (h + 1) * DK)
            queries = unit_rows(q_ref[rows, lanes].astype(F32))
            keyed = unit_rows(k_ref[rows, lanes].astype(F32))
            rate = wr_ref[rows, h : h + 1]
            summed = summed_all[:, lanes]
            middle = summed[n // 2 - 1 : n // 2, :]
            last = summed[n - 1 : n, :]
            rising = jnp.exp(summed - middle)
            key_down = keyed * jnp.exp(middle - summed)
            both = jnp.concatenate([keyed, queries], axis=0)
            lift = jnp.concatenate([rising, rising], axis=0)
            scores = dot3(both * lift, key_down, NT)
            low = jnp.where(strict, scores[:n] * rate, 0.0)
            reach = jnp.where(causal, scores[n:], 0.0)
            inv = unit_lower_inverse(low)
            grown = jnp.exp(summed)
            entry = both * jnp.concatenate([grown, grown], axis=0)
            to_end = keyed * jnp.exp(last - summed)
            decay_row = jnp.exp(last)
            decay = jnp.sum(jnp.where(eye128, decay_row, 0.0), axis=1, keepdims=True)
            prepared.append((rate, reach, inv, entry, to_end, decay))
    for c in range(PER_STEP):
        rows = slice(c * n, (c + 1) * n)
        for h in range(heads):
            lanes = slice(h * DK, (h + 1) * DK)
            rate, reach, inv, entry, to_end, decay = prepared[c * heads + h]
            state = state_ref[h]
            seen = dot3(entry, state)
            values = v_ref[rows, lanes].astype(F32)
            target = jnp.concatenate([-seen[:n, :DK], values - seen[:n, DK:]], axis=1)
            fresh = dot3(inv, target * rate)
            fh, fl = split2(fresh)
            rh, rl = split2(reach)
            ext_ref[h, rows, :] = seen[n:] + (dg(rh, fh, NN) + (dg(rh, fl, NN) + dg(rl, fh, NN)))
            eh, el = split2(to_end)
            state_ref[h] = state * decay + (
                dg(eh, fh, TN) + (dg(eh, fl, TN) + dg(el, fh, TN))
            )

    @pl.when(step == pl.num_programs(0) - 1)
    def _():
        for h in range(heads):
            state = state_ref[h]
            shifted = state[:, :DK] - jnp.where(eye128, 1.0, 0.0)
            pair_ref[h] = jnp.concatenate([shifted, state[:, DK:]], axis=1).astype(BF)


def local_chain(q, k, v, ld, wr):
    tokens, width = q.shape
    heads = wr.shape[1]
    span = CHUNK * PER_STEP
    block = pl.BlockSpec((span, width), lambda i: (i, 0))
    return pl.pallas_call(
        local_kernel,
        grid=(tokens // span,),
        in_specs=[block, block, block, block, pl.BlockSpec((span, heads), lambda i: (i, 0))],
        out_specs=[
            pl.BlockSpec((heads, span, 2 * DK), lambda i: (0, i, 0)),
            pl.BlockSpec((heads, DK, 2 * DK), lambda i: (0, 0, 0)),
        ],
        out_shape=[
            jax.ShapeDtypeStruct((heads, tokens, 2 * DK), F32),
            jax.ShapeDtypeStruct((heads, DK, 2 * DK), BF),
        ],
        scratch_shapes=[pltpu.VMEM((heads, DK, 2 * DK), F32)],
        interpret=INTERPRET,
        name="local_chain",
    )(q, k, v, ld, wr)


def prefix_kernel(place_ref, parts_ref, before_ref, total_ref):
    count, heads = parts_ref.shape[0], parts_ref.shape[1]
    place = place_ref[0]
    eye = jnp.where(iota2((DK, DK), 0) == iota2((DK, DK), 1), 1.0, 0.0)
    zero = jnp.zeros((DK, DK), F32)
    running = [jnp.concatenate([eye, zero], axis=1) for _ in range(heads)]
    kept = list(running)
    for k in range(count):
        for h in range(heads):
            part = parts_ref[k, h]
            shift = jnp.concatenate([zero, part[:, DK:].astype(F32)], axis=1)
            running[h] = running[h] + (exact_left(part[:, :DK], running[h]) + shift)
            if k + 1 < count:
                kept[h] = jnp.where(place > k, running[h], kept[h])
    for h in range(heads):
        before_ref[h] = kept[h]
        shifted = running[h][:, :DK] - eye
        total_ref[h] = jnp.concatenate([shifted, running[h][:, DK:]], axis=1).astype(BF)


def shard_prefix(place, parts):
    heads = parts.shape[1]
    shape = (heads, DK, 2 * DK)
    return pl.pallas_call(
        prefix_kernel,
        in_specs=[
            pl.BlockSpec(memory_space=pltpu.SMEM),
            pl.BlockSpec(memory_space=pltpu.VMEM),
        ],
        out_specs=[pl.BlockSpec(memory_space=pltpu.VMEM), pl.BlockSpec(memory_space=pltpu.VMEM)],
        out_shape=[jax.ShapeDtypeStruct(shape, F32), jax.ShapeDtypeStruct(shape, BF)],
        interpret=INTERPRET,
        name="shard_prefix",
    )(place, parts)


def finish_kernel(place_ref, totals_ref, before_ref, ext_ref, out_ref):
    count, heads = totals_ref.shape[0], totals_ref.shape[1]
    place = place_ref[0]
    for h in range(heads):
        state = jnp.zeros((DK, DK), F32)
        for k in range(count - 1):
            part = totals_ref[k, h]
            moved = state + (exact_left(part[:, :DK], state) + part[:, DK:].astype(F32))
            state = jnp.where(place > k, moved, state)
        before = before_ref[h]
        incoming = dot3(before[:, :DK], state) + before[:, DK:]
        ext = ext_ref[h]
        head_out = ext[:, DK:] + dot3(ext[:, :DK], incoming)
        mean = jnp.mean(head_out * head_out, axis=-1, keepdims=True)
        out_ref[:, h * DK : (h + 1) * DK] = (head_out * lax.rsqrt(mean + 1e-06)).astype(BF)


def finish_heads(place, totals, before, ext):
    heads, tokens = ext.shape[0], ext.shape[1]
    vm = pl.BlockSpec(memory_space=pltpu.VMEM)
    return pl.pallas_call(
        finish_kernel,
        in_specs=[pl.BlockSpec(memory_space=pltpu.SMEM), vm, vm, vm],
        out_specs=vm,
        out_shape=jax.ShapeDtypeStruct((tokens, heads * DK), BF),
        interpret=INTERPRET,
        name="finish_heads",
    )(place, totals, before, ext)


def turn(n, d):
    return [(i, (i + d) % n) for i in range(n)]


def ring_gather(pieces, axis):
    n = lax.axis_size(axis)
    here = lax.axis_index(axis)
    ups, downs = list(pieces), list(pieces)
    found = [{0: p} for p in pieces]
    for s in range(1, n // 2 + 1):
        for i in range(len(pieces)):
            ups[i] = lax.ppermute(ups[i], axis, turn(n, 1))
            found[i][-s] = ups[i]
            if s < n // 2:
                downs[i] = lax.ppermute(downs[i], axis, turn(n, n - 1))
                found[i][s] = downs[i]
    return found, here


def per_device(
    residual, q, k, v, log_decay, write_rate, output_weight, routes, route_gates, up, down
):
    y, z = lax.axis_index(Y), lax.axis_index(Z)
    x, core = lax.axis_index(X), lax.axis_index(C)
    ny, nz = lax.axis_size(Y), lax.axis_size(Z)
    nx, nc = lax.axis_size(X), lax.axis_size(C)
    rows = residual.shape[0]
    picks = routes.shape[1]
    width = residual.shape[1]
    ext, pair = local_chain(q, k, v, log_decay, write_rate)

    partner_weight = lax.ppermute(output_weight, C, turn(nc, 1))
    named = jnp.concatenate([routes.astype(F32), route_gates], axis=1)
    named = lax.all_gather(named, Z).reshape(nz * rows, 2 * picks)
    dests = ny * nx * nc
    dest = jnp.arange(dests, dtype=jnp.int32)
    lane_count = nx * nc
    expert_of = ((dest // lane_count) * nz + z) * lane_count + dest % lane_count
    hit = named[:, :picks, None] == expert_of[None, None, :].astype(F32)
    member = jnp.any(hit, axis=1)
    gate = jnp.sum(jnp.where(hit, named[:, picks:, None], 0.0), axis=1)
    count = nz * rows
    earlier = (
        jnp.arange(count)[:, None] > jnp.arange(count)[None, :]
    ).astype(BF)
    rank = jnp.dot(earlier, member.astype(BF), preferred_element_type=F32)
    rank = jnp.where(member, rank, -1.0)
    slot = jnp.arange(SLOTS, dtype=F32)
    chosen = (rank.T[:, None, :] == slot[None, :, None]).astype(BF).reshape(dests * SLOTS, count)
    weigh = jnp.where(rank[:, :, None] == slot[None, None, :], gate[:, :, None], 0.0)
    weigh = weigh.reshape(count, dests * SLOTS)
    weigh_hi = weigh.astype(BF)
    weigh_lo = (weigh - weigh_hi.astype(F32)).astype(BF)

    parts = lax.all_gather(pair, Z)
    before, total = shard_prefix(z.reshape(1), parts)
    totals = lax.all_gather(total, Y)
    head_norm = finish_heads(y.reshape(1), totals, before, ext)

    by_core = head_norm.reshape(nx, nc, rows, -1)
    mine = lax.dynamic_index_in_dim(by_core, core, 1, keepdims=False)
    theirs = lax.dynamic_index_in_dim(by_core, 1 - core, 1, keepdims=False)
    theirs = lax.ppermute(theirs, C, turn(nc, 1))
    partial = jnp.dot(
        mine.reshape(nx * rows, -1), output_weight, preferred_element_type=F32
    ) + jnp.dot(theirs.reshape(nx * rows, -1), partner_weight, preferred_element_type=F32)
    partial = partial.reshape(nx, rows, width)
    attended = lax.dynamic_index_in_dim(partial, x, 0, keepdims=False)
    small = partial.astype(BF)
    for d in (2, 1, 3):
        sent = lax.dynamic_index_in_dim(small, (x + d) % nx, 0, keepdims=False)
        attended = attended + lax.ppermute(sent, X, turn(nx, d)).astype(F32)
    mixed = (residual.astype(F32) + attended).astype(BF)
    mixed_wide = mixed.astype(F32)
    expert_in = (
        mixed_wide * lax.rsqrt(jnp.mean(mixed_wide * mixed_wide, axis=-1, keepdims=True) + 1e-06)
    ).astype(BF)

    column = lax.all_gather(expert_in, Z).reshape(count, width)
    outgoing = jnp.dot(chosen, column, preferred_element_type=F32).astype(BF)
    arrived = lax.all_to_all(
        outgoing.reshape(dests, SLOTS, width), PLANE, split_axis=0, concat_axis=0, tiled=True
    ).reshape(dests * SLOTS, width)
    half = down.shape[1]
    gate_up = jnp.dot(arrived, up[0], preferred_element_type=F32)
    hidden = (jax.nn.silu(gate_up[:, :half]) * gate_up[:, half:]).astype(BF)
    results = jnp.dot(hidden, down[0], preferred_element_type=F32).astype(BF)
    returned = lax.all_to_all(
        results.reshape(dests, SLOTS, width), PLANE, split_axis=0, concat_axis=0, tiled=True
    ).reshape(dests * SLOTS, width)
    combined = jnp.dot(weigh_hi, returned, preferred_element_type=F32) + jnp.dot(
        weigh_lo, returned, preferred_element_type=F32
    )
    combined = lax.psum_scatter(combined.astype(BF), Z, scatter_dimension=0, tiled=True)
    return (mixed_wide + combined.astype(F32)).astype(BF)


def solution(mesh):
    finer = Mesh(mesh.devices.reshape(4, 8, 4, 2), (Y, Z, X, C))
    seq, lanes = (Y, Z), (X, C)
    in_specs = (
        P(ALL, None),
        P(seq, lanes),
        P(seq, lanes),
        P(seq, lanes),
        P(seq, lanes),
        P(seq, lanes),
        P(lanes, None),
        P(ALL, None),
        P(ALL, None),
        P(ALL, None, None),
        P(ALL, None, None),
    )
    return jax.shard_map(
        per_device, mesh=finer, in_specs=in_specs, out_specs=P(ALL, None), check_vma=False
    )
```

```python
import jax
import jax.numpy as jnp
from jax import lax
from jax.experimental import pallas as pl
from jax.experimental.pallas import tpu as pltpu
from jax.sharding import Mesh
from jax.sharding import PartitionSpec as P

CHUNK = 64
PER_STEP = 4
DK = 128
SLOTS = 32
PIECES = 2
Z, Y, X, C = "seq_1", "seq_0", "lane", "core"
ALL = (Y, Z, X, C)
PLANE = (Y, X, C)
BF = jnp.bfloat16
F32 = jnp.float32
INTERPRET = False


def split2(x):
    hi = x.astype(BF)
    return hi, (x - hi.astype(F32)).astype(BF)


def dg(a, b, dims):
    return lax.dot_general(a, b, (dims, ((), ())), preferred_element_type=F32)


NN = ((1,), (0,))
NT = ((1,), (1,))
TN = ((0,), (0,))


def dot3(a, b, dims=NN):
    ah, al = split2(a)
    bh, bl = split2(b)
    return dot3_split(ah, al, bh, bl, dims)


def dot3_split(ah, al, bh, bl, dims=NN):
    m = ah.shape[0]
    main = dg(jnp.concatenate([ah, al], axis=0), bh, dims)
    return main[:m] + (main[m:] + dg(ah, bl, dims))


def exact_left(a, b, dims=NN):
    bh, bl = split2(b)
    return dg(a, bh, dims) + dg(a, bl, dims)


def unit_rows(x):
    return x * lax.rsqrt(jnp.sum(x * x, axis=-1, keepdims=True) + 1e-06)


def iota2(shape, dim):
    return lax.broadcasted_iota(jnp.int32, shape, dim)


def two_blocks(x, keep):
    return jnp.where(keep, jnp.concatenate([x, x], axis=0), jnp.zeros((), x.dtype))


def paired_product(a, b, keep):
    ah, al = split2(a)
    bh, bl = split2(b)
    return dot3_split(ah, al, two_blocks(bh, keep), two_blocks(bl, keep))


def unit_lower_inverses(lows, keep):
    n = CHUNK
    row, col = iota2((n, 2 * n), 0), iota2((n, 2 * n), 1) % n
    eye = jnp.where(row == col, 1.0, 0.0)
    inner = [jnp.where(row // 8 == col // 8, low, 0.0) for low in lows]
    second = [paired_product(i, i, keep) for i in inner]
    invs = [eye - i for i in inner]
    fourth = [paired_product(s, s, keep) for s in second]
    invs = [inv + paired_product(inv, s, keep) for inv, s in zip(invs, second)]
    invs = [inv + paired_product(inv, f, keep) for inv, f in zip(invs, fourth)]
    size = 16
    while size <= n:
        half = size // 2
        between = (row // size == col // size) & (row // half != col // half)
        moved = [
            paired_product(jnp.where(between, low, 0.0), inv, keep)
            for low, inv in zip(lows, invs)
        ]
        invs = [inv - paired_product(inv, m, keep) for inv, m in zip(invs, moved)]
        size *= 2
    return invs


def local_kernel(first_head, q_ref, k_ref, v_ref, ld_ref, wr_ref, ext_ref, pair_ref, state_ref):
    step = pl.program_id(0)
    n = CHUNK

    @pl.when(step == 0)
    def _():
        eye = jnp.where(iota2((DK, DK), 0) == iota2((DK, DK), 1), 1.0, 0.0)
        start = jnp.concatenate([eye, jnp.zeros((DK, DK), F32)], axis=1)
        for h in range(2):
            state_ref[h] = start

    row, col = iota2((n, 2 * n), 0), iota2((n, 2 * n), 1)
    is_first = col < n
    col = col % n
    strict, causal = row > col, row >= col
    tri = jnp.where(iota2((n, n), 0) >= iota2((n, n), 1), 1.0, 0.0).astype(BF)
    keep = (iota2((2 * n, 2 * n), 0) < n) == (iota2((2 * n, 2 * n), 1) < n)
    eye128 = iota2((DK, DK), 0) == iota2((DK, DK), 1)
    lows, reaches, details = [], [], []
    for c in range(PER_STEP):
        rows = slice(c * n, (c + 1) * n)
        logs = ld_ref[rows, :]
        one = logs.astype(BF)
        two, three = split2(logs - one.astype(F32))
        summed_all = dg(tri, one, NN) + (dg(tri, two, NN) + dg(tri, three, NN))
        lifted, downs, kept = [], [], []
        for h in range(2):
            lanes = slice(h * DK, (h + 1) * DK)
            queries = unit_rows(q_ref[rows, lanes].astype(F32))
            keyed = unit_rows(k_ref[rows, lanes].astype(F32))
            rate = wr_ref[rows, first_head + h : first_head + h + 1]
            summed = summed_all[:, lanes]
            middle = summed[n // 2 - 1 : n // 2, :]
            last = summed[n - 1 : n, :]
            rising = jnp.exp(summed - middle)
            downs.append(keyed * jnp.exp(middle - summed))
            lifted.append(jnp.concatenate([keyed * rising, queries * rising], axis=0))
            grown = jnp.exp(summed)
            entry = jnp.concatenate([keyed * grown, queries * grown], axis=0)
            to_end = keyed * jnp.exp(last - summed)
            decay = jnp.sum(jnp.where(eye128, jnp.exp(last), 0.0), axis=1, keepdims=True)
            kept.append((rate, entry, to_end, decay))
        down_h, down_l = split2(jnp.concatenate(downs, axis=0))
        scores = []
        for h in range(2):
            lh, ll = split2(lifted[h])
            scores.append(dot3_split(lh, ll, down_h, down_l, NT))
        rates = jnp.where(is_first, kept[0][0], kept[1][0])
        key_part = jnp.where(is_first, scores[0][:n], scores[1][:n])
        query_part = jnp.where(is_first, scores[0][n:], scores[1][n:])
        lows.append(jnp.where(strict, key_part * rates, 0.0))
        reaches.append(jnp.where(causal, query_part, 0.0))
        details.append(kept)
    invs = unit_lower_inverses(lows, keep)
    for c in range(PER_STEP):
        rows = slice(c * n, (c + 1) * n)
        states, targets, seen_out = [], [], []
        for h in range(2):
            rate, entry, to_end, decay = details[c][h]
            state = state_ref[h]
            seen = dot3(entry, state)
            values = v_ref[rows, h * DK : (h + 1) * DK].astype(F32)
            target = jnp.concatenate([-seen[:n, :DK], values - seen[:n, DK:]], axis=1)
            targets.append(target * rate)
            states.append(state)
            seen_out.append(seen[n:])
        ih, il = split2(invs[c])
        th, tl = split2(jnp.concatenate(targets, axis=0))
        fresh = dot3_split(two_blocks(ih, keep), two_blocks(il, keep), th, tl)
        fh, fl = split2(fresh)
        rh, rl = split2(reaches[c])
        spread = dot3_split(two_blocks(rh, keep), two_blocks(rl, keep), fh, fl)
        for h in range(2):
            rate, entry, to_end, decay = details[c][h]
            part = slice(h * n, (h + 1) * n)
            ext_ref[h, rows, :] = seen_out[h] + spread[part]
            eh, el = split2(to_end)
            state_ref[h] = states[h] * decay + (
                dg(eh, fh[part], TN) + (dg(eh, fl[part], TN) + dg(el, fh[part], TN))
            )

    @pl.when(step == pl.num_programs(0) - 1)
    def _():
        for h in range(2):
            state = state_ref[h]
            shifted = state[:, :DK] - jnp.where(eye128, 1.0, 0.0)
            pair_ref[h] = jnp.concatenate([shifted, state[:, DK:]], axis=1).astype(BF)


def local_chain(q, k, v, ld, wr, group):
    tokens = q.shape[0]
    heads = wr.shape[1]
    span = CHUNK * PER_STEP
    block = pl.BlockSpec((span, 2 * DK), lambda i: (i, group))

    def kernel(*refs):
        local_kernel(2 * group, *refs)

    return pl.pallas_call(
        kernel,
        grid=(tokens // span,),
        in_specs=[block, block, block, block, pl.BlockSpec((span, heads), lambda i: (i, 0))],
        out_specs=[
            pl.BlockSpec((2, span, 2 * DK), lambda i: (0, i, 0)),
            pl.BlockSpec((2, DK, 2 * DK), lambda i: (0, 0, 0)),
        ],
        out_shape=[
            jax.ShapeDtypeStruct((2, tokens, 2 * DK), F32),
            jax.ShapeDtypeStruct((2, DK, 2 * DK), BF),
        ],
        scratch_shapes=[pltpu.VMEM((2, DK, 2 * DK), F32)],
        interpret=INTERPRET,
        name="local_chain",
    )(q, k, v, ld, wr)


def prefix_kernel(place_ref, parts_ref, before_ref, total_ref):
    count, heads = parts_ref.shape[0], parts_ref.shape[1]
    place = place_ref[0]
    eye = jnp.where(iota2((DK, DK), 0) == iota2((DK, DK), 1), 1.0, 0.0)
    zero = jnp.zeros((DK, DK), F32)
    running = [jnp.concatenate([eye, zero], axis=1) for _ in range(heads)]
    kept = list(running)
    for k in range(count):
        for h in range(heads):
            part = parts_ref[k, h]
            shift = jnp.concatenate([zero, part[:, DK:].astype(F32)], axis=1)
            running[h] = running[h] + (exact_left(part[:, :DK], running[h]) + shift)
            if k + 1 < count:
                kept[h] = jnp.where(place > k, running[h], kept[h])
    for h in range(heads):
        before_ref[h] = kept[h]
        shifted = running[h][:, :DK] - eye
        total_ref[h] = jnp.concatenate([shifted, running[h][:, DK:]], axis=1).astype(BF)


def shard_prefix(place, parts):
    heads = parts.shape[1]
    shape = (heads, DK, 2 * DK)
    return pl.pallas_call(
        prefix_kernel,
        in_specs=[
            pl.BlockSpec(memory_space=pltpu.SMEM),
            pl.BlockSpec(memory_space=pltpu.VMEM),
        ],
        out_specs=[pl.BlockSpec(memory_space=pltpu.VMEM), pl.BlockSpec(memory_space=pltpu.VMEM)],
        out_shape=[jax.ShapeDtypeStruct(shape, F32), jax.ShapeDtypeStruct(shape, BF)],
        interpret=INTERPRET,
        name="shard_prefix",
    )(place, parts)


def finish_kernel(place_ref, *refs):
    totals, (before_ref, ext_ref, out_ref) = refs[:-3], refs[-3:]
    heads = ext_ref.shape[0]
    place = place_ref[0]
    for h in range(heads):
        state = jnp.zeros((DK, DK), F32)
        for i, total_ref in enumerate(totals):
            part = total_ref[h]
            moved = state + (exact_left(part[:, :DK], state) + part[:, DK:].astype(F32))
            state = jnp.where(place >= len(totals) - i, moved, state)
        before = before_ref[h]
        incoming = dot3(before[:, :DK], state) + before[:, DK:]
        ext = ext_ref[h]
        head_out = ext[:, DK:] + dot3(ext[:, :DK], incoming)
        mean = jnp.mean(head_out * head_out, axis=-1, keepdims=True)
        out_ref[:, h * DK : (h + 1) * DK] = (head_out * lax.rsqrt(mean + 1e-06)).astype(BF)


def finish_heads(place, totals, before, ext):
    heads, tokens = ext.shape[0], ext.shape[1]
    vm = pl.BlockSpec(memory_space=pltpu.VMEM)
    return pl.pallas_call(
        finish_kernel,
        in_specs=[pl.BlockSpec(memory_space=pltpu.SMEM)] + [vm] * (len(totals) + 2),
        out_specs=vm,
        out_shape=jax.ShapeDtypeStruct((tokens, heads * DK), BF),
        interpret=INTERPRET,
        name="finish_heads",
    )(place, *totals, before, ext)


def turn(n, d):
    return [(i, (i + d) % n) for i in range(n)]


def exchange(x, dests):
    width = x.shape[1]
    return lax.all_to_all(
        x.reshape(dests, SLOTS, width), PLANE, split_axis=0, concat_axis=0, tiled=True
    ).reshape(dests * SLOTS, width)


def routing_tables(routes, route_gates, after, z, nz, dests, lane_count):
    rows, picks = routes.shape
    pad = jnp.zeros((rows, DK - 2 * picks), F32)
    named = jnp.concatenate([routes.astype(F32), route_gates, pad], axis=1)
    named, after = lax.optimization_barrier((named, after))
    shifted = [lax.ppermute(named, Z, turn(nz, d)) for d in range(nz - 1, 0, -1)] + [named]
    ordered = jnp.concatenate(shifted + shifted[:-1], axis=0)
    count = nz * rows
    ordered = lax.dynamic_slice_in_dim(ordered, (nz - 1 - z) * rows, count, 0)
    dest = jnp.arange(dests, dtype=jnp.int32)
    expert_of = ((dest // lane_count) * nz + z) * lane_count + dest % lane_count
    hit = ordered[:, :picks, None] == expert_of[None, None, :].astype(F32)
    member = jnp.any(hit, axis=1)
    gate = jnp.sum(jnp.where(hit, ordered[:, picks : 2 * picks, None], 0.0), axis=1)
    earlier = (jnp.arange(count)[:, None] > jnp.arange(count)[None, :]).astype(BF)
    rank = jnp.dot(earlier, member.astype(BF), preferred_element_type=F32)
    rank = jnp.where(member, rank, -1.0)
    slot = jnp.arange(SLOTS, dtype=F32)
    chosen = (rank.T[:, None, :] == slot[None, :, None]).astype(BF).reshape(dests * SLOTS, count)
    weigh = jnp.where(rank[:, :, None] == slot[None, None, :], gate[:, :, None], 0.0)
    weigh = weigh.reshape(count, dests * SLOTS)
    weigh_hi = weigh.astype(BF)
    weigh_lo = (weigh - weigh_hi.astype(F32)).astype(BF)
    return (chosen, weigh_hi, weigh_lo), after


def per_device(
    residual, q, k, v, log_decay, write_rate, output_weight, routes, route_gates, up, down
):
    y, z = lax.axis_index(Y), lax.axis_index(Z)
    x, core = lax.axis_index(X), lax.axis_index(C)
    ny, nz = lax.axis_size(Y), lax.axis_size(Z)
    nx, nc = lax.axis_size(X), lax.axis_size(C)
    rows = residual.shape[0]
    width = residual.shape[1]
    partner_weight = lax.ppermute(output_weight, C, turn(nc, 1))
    weights = jnp.concatenate([output_weight, partner_weight], axis=0)
    dests, count = ny * nx * nc, nz * rows
    norms = []
    for group in range(2):
        ext, pair = local_chain(q, k, v, log_decay, write_rate, group)
        if group == 1:
            tables, pair = routing_tables(
                routes, route_gates, pair, z, nz, dests, nx * nc
            )
        parts = lax.all_gather(pair, Z)
        if group == 1:
            parts, tables = lax.optimization_barrier((parts, tables))
        before, total = shard_prefix(z.reshape(1), parts)
        totals = [lax.ppermute(total, Y, turn(ny, d)) for d in range(ny - 1, 0, -1)]
        norms.append(finish_heads(y.reshape(1), totals, before, ext))
    head_norm = jnp.concatenate(norms, axis=1)
    chosen, weigh_hi, weigh_lo = tables

    by_core = head_norm.reshape(nx, nc, rows, -1)
    mine = lax.dynamic_index_in_dim(by_core, core, 1, keepdims=False)
    theirs = lax.dynamic_index_in_dim(by_core, 1 - core, 1, keepdims=False)
    theirs = lax.ppermute(theirs, C, turn(nc, 1))
    both = jnp.concatenate([mine, theirs], axis=-1).reshape(nx * rows, -1)
    partial = jnp.dot(both, weights, preferred_element_type=F32).reshape(nx, rows, width)
    attended = lax.dynamic_index_in_dim(partial, x, 0, keepdims=False)
    small = partial.astype(BF)
    for d in (2, 1, 3):
        sent = lax.dynamic_index_in_dim(small, (x + d) % nx, 0, keepdims=False)
        attended = attended + lax.ppermute(sent, X, turn(nx, d)).astype(F32)
    mixed = (residual.astype(F32) + attended).astype(BF)
    mixed_wide = mixed.astype(F32)
    expert_in = (
        mixed_wide * lax.rsqrt(jnp.mean(mixed_wide * mixed_wide, axis=-1, keepdims=True) + 1e-06)
    ).astype(BF)

    half = down.shape[1]
    piece = width // PIECES
    columns = [slice(i * piece, (i + 1) * piece) for i in range(PIECES)]
    gate_up = jnp.zeros((dests * SLOTS, 2 * half), F32)
    token = None
    for cols in columns:
        sent = expert_in[:, cols]
        if token is not None:
            sent, token = lax.optimization_barrier((sent, token))
        token = lax.all_gather(sent, Z)
        outgoing = jnp.dot(
            chosen, token.reshape(count, piece), preferred_element_type=F32
        ).astype(BF)
        arrived = exchange(outgoing, dests)
        gate_up = gate_up + jnp.dot(arrived, up[0][cols], preferred_element_type=F32)
    hidden = (jax.nn.silu(gate_up[:, :half]) * gate_up[:, half:]).astype(BF)
    outs = []
    combined = None
    for cols in columns:
        results = jnp.dot(hidden, down[0][:, cols], preferred_element_type=F32).astype(BF)
        if combined is not None:
            results, combined = lax.optimization_barrier((results, combined))
            outs.append(lax.psum_scatter(combined, Z, scatter_dimension=0, tiled=True))
        returned = exchange(results, dests)
        combined = (
            jnp.dot(weigh_hi, returned, preferred_element_type=F32)
            + jnp.dot(weigh_lo, returned, preferred_element_type=F32)
        ).astype(BF)
    outs.append(lax.psum_scatter(combined, Z, scatter_dimension=0, tiled=True))
    return (mixed_wide + jnp.concatenate(outs, axis=1).astype(F32)).astype(BF)


def solution(mesh):
    finer = Mesh(mesh.devices.reshape(4, 8, 4, 2), (Y, Z, X, C))
    seq, lanes = (Y, Z), (X, C)
    in_specs = (
        P(ALL, None),
        P(seq, lanes),
        P(seq, lanes),
        P(seq, lanes),
        P(seq, lanes),
        P(seq, lanes),
        P(lanes, None),
        P(ALL, None),
        P(ALL, None),
        P(ALL, None, None),
        P(ALL, None, None),
    )
    return jax.shard_map(
        per_device, mesh=finer, in_specs=in_specs, out_specs=P(ALL, None), check_vma=False
    )
```

```python
import jax
import jax.numpy as jnp
from jax import lax
from jax.experimental import pallas as pl
from jax.experimental.pallas import tpu as pltpu
from jax.sharding import Mesh
from jax.sharding import PartitionSpec as P

CHUNK = 64
PER_STEP = 4
DK = 128
SLOTS = 32
Z, Y, X, C = "seq_1", "seq_0", "lane", "core"
ALL = (Y, Z, X, C)
PLANE = (Y, X, C)
BF = jnp.bfloat16
F32 = jnp.float32
INTERPRET = False


def split2(x):
    hi = x.astype(BF)
    return hi, (x - hi.astype(F32)).astype(BF)


def dg(a, b, dims):
    return lax.dot_general(a, b, (dims, ((), ())), preferred_element_type=F32)


NN = ((1,), (0,))
NT = ((1,), (1,))
TN = ((0,), (0,))


def dot3(a, b, dims=NN):
    ah, al = split2(a)
    bh, bl = split2(b)
    return dot3_split(ah, al, bh, bl, dims)


def dot3_split(ah, al, bh, bl, dims=NN):
    m = ah.shape[0]
    main = dg(jnp.concatenate([ah, al], axis=0), bh, dims)
    return main[:m] + (main[m:] + dg(ah, bl, dims))


def exact_left(a, b, dims=NN):
    bh, bl = split2(b)
    return dg(a, bh, dims) + dg(a, bl, dims)


def unit_rows(x):
    return x * lax.rsqrt(jnp.sum(x * x, axis=-1, keepdims=True) + 1e-06)


def iota2(shape, dim):
    return lax.broadcasted_iota(jnp.int32, shape, dim)


def two_blocks(x, keep):
    return jnp.where(keep, jnp.concatenate([x, x], axis=0), jnp.zeros((), x.dtype))


def paired_product(a, b, keep):
    ah, al = split2(a)
    bh, bl = split2(b)
    return dot3_split(ah, al, two_blocks(bh, keep), two_blocks(bl, keep))


def unit_lower_inverses(lows, keep):
    n = CHUNK
    row, col = iota2((n, 2 * n), 0), iota2((n, 2 * n), 1) % n
    eye = jnp.where(row == col, 1.0, 0.0)
    inner = [jnp.where(row // 8 == col // 8, low, 0.0) for low in lows]
    second = [paired_product(i, i, keep) for i in inner]
    invs = [eye - i for i in inner]
    fourth = [paired_product(s, s, keep) for s in second]
    invs = [inv + paired_product(inv, s, keep) for inv, s in zip(invs, second)]
    invs = [inv + paired_product(inv, f, keep) for inv, f in zip(invs, fourth)]
    size = 16
    while size <= n:
        half = size // 2
        between = (row // size == col // size) & (row // half != col // half)
        moved = [
            paired_product(jnp.where(between, low, 0.0), inv, keep)
            for low, inv in zip(lows, invs)
        ]
        invs = [inv - paired_product(inv, m, keep) for inv, m in zip(invs, moved)]
        size *= 2
    return invs


def local_kernel(first_head, q_ref, k_ref, v_ref, ld_ref, wr_ref, ext_ref, pair_ref, state_ref):
    step = pl.program_id(0)
    n = CHUNK

    @pl.when(step == 0)
    def _():
        eye = jnp.where(iota2((DK, DK), 0) == iota2((DK, DK), 1), 1.0, 0.0)
        start = jnp.concatenate([eye, jnp.zeros((DK, DK), F32)], axis=1)
        for h in range(2):
            state_ref[h] = start

    row, col = iota2((n, 2 * n), 0), iota2((n, 2 * n), 1)
    is_first = col < n
    col = col % n
    strict, causal = row > col, row >= col
    tri = jnp.where(iota2((n, n), 0) >= iota2((n, n), 1), 1.0, 0.0).astype(BF)
    keep = (iota2((2 * n, 2 * n), 0) < n) == (iota2((2 * n, 2 * n), 1) < n)
    eye128 = iota2((DK, DK), 0) == iota2((DK, DK), 1)
    lows, reaches, details = [], [], []
    for c in range(PER_STEP):
        rows = slice(c * n, (c + 1) * n)
        logs = ld_ref[rows, :]
        one = logs.astype(BF)
        two, three = split2(logs - one.astype(F32))
        summed_all = dg(tri, one, NN) + (dg(tri, two, NN) + dg(tri, three, NN))
        lifted, downs, kept = [], [], []
        for h in range(2):
            lanes = slice(h * DK, (h + 1) * DK)
            queries = unit_rows(q_ref[rows, lanes].astype(F32))
            keyed = unit_rows(k_ref[rows, lanes].astype(F32))
            rate = wr_ref[rows, first_head + h : first_head + h + 1]
            summed = summed_all[:, lanes]
            middle = summed[n // 2 - 1 : n // 2, :]
            last = summed[n - 1 : n, :]
            rising = jnp.exp(summed - middle)
            downs.append(keyed * jnp.exp(middle - summed))
            lifted.append(jnp.concatenate([keyed * rising, queries * rising], axis=0))
            grown = jnp.exp(summed)
            entry = jnp.concatenate([keyed * grown, queries * grown], axis=0)
            to_end = keyed * jnp.exp(last - summed)
            decay = jnp.sum(jnp.where(eye128, jnp.exp(last), 0.0), axis=1, keepdims=True)
            kept.append((rate, entry, to_end, decay))
        down_h, down_l = split2(jnp.concatenate(downs, axis=0))
        scores = []
        for h in range(2):
            lh, ll = split2(lifted[h])
            scores.append(dot3_split(lh, ll, down_h, down_l, NT))
        rates = jnp.where(is_first, kept[0][0], kept[1][0])
        key_part = jnp.where(is_first, scores[0][:n], scores[1][:n])
        query_part = jnp.where(is_first, scores[0][n:], scores[1][n:])
        lows.append(jnp.where(strict, key_part * rates, 0.0))
        reaches.append(jnp.where(causal, query_part, 0.0))
        details.append(kept)
    invs = unit_lower_inverses(lows, keep)
    for c in range(PER_STEP):
        rows = slice(c * n, (c + 1) * n)
        states, targets, seen_out = [], [], []
        for h in range(2):
            rate, entry, to_end, decay = details[c][h]
            state = state_ref[h]
            seen = dot3(entry, state)
            values = v_ref[rows, h * DK : (h + 1) * DK].astype(F32)
            target = jnp.concatenate([-seen[:n, :DK], values - seen[:n, DK:]], axis=1)
            targets.append(target * rate)
            states.append(state)
            seen_out.append(seen[n:])
        ih, il = split2(invs[c])
        th, tl = split2(jnp.concatenate(targets, axis=0))
        fresh = dot3_split(two_blocks(ih, keep), two_blocks(il, keep), th, tl)
        fh, fl = split2(fresh)
        rh, rl = split2(reaches[c])
        spread = dot3_split(two_blocks(rh, keep), two_blocks(rl, keep), fh, fl)
        for h in range(2):
            rate, entry, to_end, decay = details[c][h]
            part = slice(h * n, (h + 1) * n)
            ext_ref[h, rows, :] = seen_out[h] + spread[part]
            eh, el = split2(to_end)
            state_ref[h] = states[h] * decay + (
                dg(eh, fh[part], TN) + (dg(eh, fl[part], TN) + dg(el, fh[part], TN))
            )

    @pl.when(step == pl.num_programs(0) - 1)
    def _():
        for h in range(2):
            state = state_ref[h]
            shifted = state[:, :DK] - jnp.where(eye128, 1.0, 0.0)
            pair_ref[h] = jnp.concatenate([shifted, state[:, DK:]], axis=1).astype(BF)


def local_chain(q, k, v, ld, wr, group):
    tokens = q.shape[0]
    heads = wr.shape[1]
    span = CHUNK * PER_STEP
    block = pl.BlockSpec((span, 2 * DK), lambda i: (i, group))

    def kernel(*refs):
        local_kernel(2 * group, *refs)

    return pl.pallas_call(
        kernel,
        grid=(tokens // span,),
        in_specs=[block, block, block, block, pl.BlockSpec((span, heads), lambda i: (i, 0))],
        out_specs=[
            pl.BlockSpec((2, span, 2 * DK), lambda i: (0, i, 0)),
            pl.BlockSpec((2, DK, 2 * DK), lambda i: (0, 0, 0)),
        ],
        out_shape=[
            jax.ShapeDtypeStruct((2, tokens, 2 * DK), F32),
            jax.ShapeDtypeStruct((2, DK, 2 * DK), BF),
        ],
        scratch_shapes=[pltpu.VMEM((2, DK, 2 * DK), F32)],
        interpret=INTERPRET,
        name="local_chain",
    )(q, k, v, ld, wr)


def prefix_kernel(place_ref, *refs):
    sources, (before_ref, total_ref, parts_ref) = refs[:-3], refs[-3:]
    count, heads = parts_ref.shape[0], before_ref.shape[0]
    place = place_ref[0]
    for i, source_ref in enumerate(sources):
        parts_ref[i] = source_ref[: heads * DK, :]
    eye = jnp.where(iota2((DK, DK), 0) == iota2((DK, DK), 1), 1.0, 0.0)
    zero = jnp.zeros((DK, DK), F32)
    running = [jnp.concatenate([eye, zero], axis=1) for _ in range(heads)]
    kept = list(running)
    for k in range(count):
        source = lax.rem(k - place + count, count)
        for h in range(heads):
            part = parts_ref[source, h * DK : (h + 1) * DK, :]
            shift = jnp.concatenate([zero, part[:, DK:].astype(F32)], axis=1)
            running[h] = running[h] + (exact_left(part[:, :DK], running[h]) + shift)
            if k + 1 < count:
                kept[h] = jnp.where(place > k, running[h], kept[h])
    for h in range(heads):
        before_ref[h] = kept[h]
        shifted = running[h][:, :DK] - eye
        total_ref[h] = jnp.concatenate([shifted, running[h][:, DK:]], axis=1).astype(BF)


def shard_prefix(place, parts):
    shape = (2, DK, 2 * DK)
    return pl.pallas_call(
        prefix_kernel,
        in_specs=[pl.BlockSpec(memory_space=pltpu.SMEM)]
        + [pl.BlockSpec(memory_space=pltpu.VMEM)] * len(parts),
        out_specs=[pl.BlockSpec(memory_space=pltpu.VMEM), pl.BlockSpec(memory_space=pltpu.VMEM)],
        out_shape=[jax.ShapeDtypeStruct(shape, F32), jax.ShapeDtypeStruct(shape, BF)],
        scratch_shapes=[pltpu.VMEM((len(parts), 2 * DK, 2 * DK), BF)],
        interpret=INTERPRET,
        name="shard_prefix",
    )(place, *parts)


def finish_kernel(place_ref, *refs):
    totals, befores, exts, out_ref = refs[:-5], refs[-5:-3], refs[-3:-1], refs[-1]
    place = place_ref[0]
    for h in range(4):
        state = jnp.zeros((DK, DK), F32)
        for i, total_ref in enumerate(totals):
            part = total_ref[h]
            moved = state + (exact_left(part[:, :DK], state) + part[:, DK:].astype(F32))
            state = jnp.where(place >= len(totals) - i, moved, state)
        before = befores[h // 2][h % 2]
        incoming = dot3(before[:, :DK], state) + before[:, DK:]
        ext = exts[h // 2][h % 2]
        head_out = ext[:, DK:] + dot3(ext[:, :DK], incoming)
        mean = jnp.mean(head_out * head_out, axis=-1, keepdims=True)
        out_ref[:, h * DK : (h + 1) * DK] = (head_out * lax.rsqrt(mean + 1e-06)).astype(BF)


def finish_heads(place, totals, befores, exts):
    tokens = exts[0].shape[1]
    vm = pl.BlockSpec(memory_space=pltpu.VMEM)
    return pl.pallas_call(
        finish_kernel,
        in_specs=[pl.BlockSpec(memory_space=pltpu.SMEM)] + [vm] * (len(totals) + 4),
        out_specs=vm,
        out_shape=jax.ShapeDtypeStruct((tokens, 4 * DK), BF),
        interpret=INTERPRET,
        name="finish_heads",
    )(place, *totals, *befores, *exts)


def turn(n, d):
    return [(i, (i + d) % n) for i in range(n)]


def exchange(x, dests):
    width = x.shape[1]
    return lax.all_to_all(
        x.reshape(dests, SLOTS, width), PLANE, split_axis=0, concat_axis=0, tiled=True
    ).reshape(dests * SLOTS, width)


def ring_gather(own, axis):
    n = lax.axis_size(axis)
    found = [None] * n
    found[0] = up = down = own
    for s in range(1, n // 2 + 1):
        up = lax.ppermute(up, axis, turn(n, 1))
        found[n - s] = up
        if s < n // 2:
            down = lax.ppermute(down, axis, turn(n, n - 1))
            found[s] = down
    return found


def ring_reduce(parts, axis):
    n = len(parts)
    half = n // 2
    up, down = parts[half], parts[half + 1]
    for s in range(half, 0, -1):
        up = lax.ppermute(up, axis, turn(n, 1)).astype(F32)
        if s > 1:
            up = (up + parts[s - 1].astype(F32)).astype(BF)
        if s > 1:
            down = lax.ppermute(down, axis, turn(n, n - 1)).astype(F32)
            if s > 2:
                down = (down + parts[n + 1 - s + 1].astype(F32)).astype(BF)
    return up + down + parts[0].astype(F32)


def routing_info(routes, route_gates):
    rows, picks = routes.shape
    high, low = split2(route_gates)
    pad = jnp.zeros((rows, picks), BF)
    info = jnp.concatenate([routes.astype(BF), high, low, pad], axis=1)
    info = info.reshape(rows * picks * 4 // (2 * DK), 2 * DK)
    return jnp.concatenate([info, jnp.zeros_like(info)], axis=0)


def routing_tables(info, picks, z, nz, dests, lane_count):
    count = info.shape[0]
    info = info.astype(F32)
    routes = info[:, :picks]
    gates = info[:, picks : 2 * picks] + info[:, 2 * picks : 3 * picks]
    dest = jnp.arange(dests, dtype=jnp.int32)
    expert_of = ((dest // lane_count) * nz + z) * lane_count + dest % lane_count
    hit = routes[:, :, None] == expert_of[None, None, :].astype(F32)
    member = jnp.any(hit, axis=1)
    gate = jnp.sum(jnp.where(hit, gates[:, :, None], 0.0), axis=1)
    earlier = (jnp.arange(count)[:, None] > jnp.arange(count)[None, :]).astype(BF)
    rank = jnp.dot(earlier, member.astype(BF), preferred_element_type=F32)
    rank = jnp.where(member, rank, -1.0)
    slot = jnp.arange(SLOTS, dtype=F32)
    chosen = (rank.T[:, None, :] == slot[None, :, None]).astype(BF).reshape(dests * SLOTS, count)
    weigh = jnp.where(rank[:, :, None] == slot[None, None, :], gate[:, :, None], 0.0)
    weigh = weigh.reshape(count, dests * SLOTS)
    weigh_hi = weigh.astype(BF)
    weigh_lo = (weigh - weigh_hi.astype(F32)).astype(BF)
    return chosen, weigh_hi, weigh_lo


def exchange(x, dests):
    width = x.shape[1]
    return lax.all_to_all(
        x.reshape(dests, SLOTS, width), PLANE, split_axis=0, concat_axis=0, tiled=True
    ).reshape(dests * SLOTS, width)


def per_device(
    residual, q, k, v, log_decay, write_rate, output_weight, routes, route_gates, up, down
):
    y, z = lax.axis_index(Y), lax.axis_index(Z)
    x, core = lax.axis_index(X), lax.axis_index(C)
    ny, nz = lax.axis_size(Y), lax.axis_size(Z)
    nx, nc = lax.axis_size(X), lax.axis_size(C)
    rows, width = residual.shape
    picks = routes.shape[1]
    dests, count = ny * nx * nc, nz * rows

    partner_weight = lax.ppermute(output_weight, C, turn(nc, 1))
    weights = jnp.concatenate([output_weight, partner_weight], axis=0)
    info = routing_info(routes, route_gates)
    exts, befores, totals = [], [], []
    for group in range(2):
        ext, pair = local_chain(q, k, v, log_decay, write_rate, group)
        load = pair.reshape(2 * DK, 2 * DK)
        if group == 0:
            load = jnp.concatenate([load, info], axis=0)
        parts = ring_gather(load, Z)
        if group == 0:
            named = slice(2 * DK, 2 * DK + info.shape[0] // 2)
            shared = jnp.concatenate(
                [part[named].reshape(rows, 4 * picks) for part in parts], axis=0
            )
        before, total = shard_prefix(z.reshape(1), parts)
        exts.append(ext)
        befores.append(before)
        totals.append(total)
    total = jnp.concatenate(totals, axis=0)
    tables = routing_tables(shared, picks, z, nz, dests, nx * nc)
    earlier = [lax.ppermute(total, Y, turn(ny, d)) for d in range(ny - 1, 0, -1)]
    earlier, tables = lax.optimization_barrier((earlier, tables))
    chosen, weigh_hi, weigh_lo = tables
    head_norm = finish_heads(y.reshape(1), earlier, befores, exts)

    by_core = head_norm.reshape(nx, nc, rows, -1)
    mine = lax.dynamic_index_in_dim(by_core, core, 1, keepdims=False)
    theirs = lax.dynamic_index_in_dim(by_core, 1 - core, 1, keepdims=False)
    theirs = lax.ppermute(theirs, C, turn(nc, 1))
    both = jnp.concatenate([mine, theirs], axis=-1).reshape(nx * rows, -1)
    partial = jnp.dot(both, weights, preferred_element_type=F32).reshape(nx, rows, width)
    attended = lax.dynamic_index_in_dim(partial, x, 0, keepdims=False)
    small = partial.astype(BF)
    for d in (2, 1, 3):
        sent = lax.dynamic_index_in_dim(small, (x + d) % nx, 0, keepdims=False)
        attended = attended + lax.ppermute(sent, X, turn(nx, d)).astype(F32)
    mixed = (residual.astype(F32) + attended).astype(BF)
    mixed_wide = mixed.astype(F32)
    expert_in = (
        mixed_wide * lax.rsqrt(jnp.mean(mixed_wide * mixed_wide, axis=-1, keepdims=True) + 1e-06)
    ).astype(BF)

    cut = width // 2
    left = jnp.concatenate(ring_gather(expert_in[:, :cut], Z), axis=0)
    right = jnp.concatenate(ring_gather(expert_in[:, cut:], Z), axis=0)
    column = jnp.concatenate([left, right], axis=1)
    outgoing = jnp.dot(chosen, column, preferred_element_type=F32).astype(BF)
    arrived = exchange(outgoing, dests)
    half = down.shape[1]
    gate_up = jnp.dot(arrived, up[0], preferred_element_type=F32)
    hidden = (jax.nn.silu(gate_up[:, :half]) * gate_up[:, half:]).astype(BF)
    results = jnp.dot(hidden, down[0], preferred_element_type=F32).astype(BF)
    returned = exchange(results, dests)
    combined = (
        jnp.dot(weigh_hi, returned, preferred_element_type=F32)
        + jnp.dot(weigh_lo, returned, preferred_element_type=F32)
    ).astype(BF)
    combined = combined.reshape(nz, rows, width)
    outs = [
        ring_reduce([combined[r][:, cols] for r in range(nz)], Z)
        for cols in (slice(0, cut), slice(cut, width))
    ]
    return (mixed_wide + jnp.concatenate(outs, axis=1)).astype(BF)


def solution(mesh):
    finer = Mesh(mesh.devices.reshape(4, 8, 4, 2), (Y, Z, X, C))
    seq, lanes = (Y, Z), (X, C)
    in_specs = (
        P(ALL, None),
        P(seq, lanes),
        P(seq, lanes),
        P(seq, lanes),
        P(seq, lanes),
        P(seq, lanes),
        P(lanes, None),
        P(ALL, None),
        P(ALL, None),
        P(ALL, None, None),
        P(ALL, None, None),
    )
    return jax.shard_map(
        per_device, mesh=finer, in_specs=in_specs, out_specs=P(ALL, None), check_vma=False
    )
```

```python
import jax
import jax.numpy as jnp
from jax import lax
from jax.experimental import pallas as pl
from jax.experimental.pallas import tpu as pltpu
from jax.sharding import Mesh
from jax.sharding import PartitionSpec as P

CHUNK = 64
PER_STEP = 4
DK = 128
SLOTS = 32
CUT = 1024
Z, Y, X, C = "seq_1", "seq_0", "lane", "core"
ALL = (Y, Z, X, C)
PLANE = (Y, X, C)
BF = jnp.bfloat16
F32 = jnp.float32
INTERPRET = False


def split2(x):
    hi = x.astype(BF)
    return hi, (x - hi.astype(F32)).astype(BF)


def dg(a, b, dims):
    return lax.dot_general(a, b, (dims, ((), ())), preferred_element_type=F32)


NN = ((1,), (0,))
NT = ((1,), (1,))
TN = ((0,), (0,))


def dot3(a, b, dims=NN):
    ah, al = split2(a)
    bh, bl = split2(b)
    return dot3_split(ah, al, bh, bl, dims)


def dot3_split(ah, al, bh, bl, dims=NN):
    m = ah.shape[0]
    main = dg(jnp.concatenate([ah, al], axis=0), bh, dims)
    return main[:m] + (main[m:] + dg(ah, bl, dims))


def exact_left(a, b, dims=NN):
    bh, bl = split2(b)
    return dg(a, bh, dims) + dg(a, bl, dims)


def unit_rows(x):
    return x * lax.rsqrt(jnp.sum(x * x, axis=-1, keepdims=True) + 1e-06)


def iota2(shape, dim):
    return lax.broadcasted_iota(jnp.int32, shape, dim)


def two_blocks(x, keep):
    return jnp.where(keep, jnp.concatenate([x, x], axis=0), jnp.zeros((), x.dtype))


def paired_product(a, b, keep):
    ah, al = split2(a)
    bh, bl = split2(b)
    return dot3_split(ah, al, two_blocks(bh, keep), two_blocks(bl, keep))


def unit_lower_inverses(lows, keep):
    n = CHUNK
    row, col = iota2((n, 2 * n), 0), iota2((n, 2 * n), 1) % n
    eye = jnp.where(row == col, 1.0, 0.0)
    inner = [jnp.where(row // 8 == col // 8, low, 0.0) for low in lows]
    second = [paired_product(i, i, keep) for i in inner]
    invs = [eye - i for i in inner]
    fourth = [paired_product(s, s, keep) for s in second]
    invs = [inv + paired_product(inv, s, keep) for inv, s in zip(invs, second)]
    invs = [inv + paired_product(inv, f, keep) for inv, f in zip(invs, fourth)]
    size = 16
    while size <= n:
        half = size // 2
        between = (row // size == col // size) & (row // half != col // half)
        moved = [
            paired_product(jnp.where(between, low, 0.0), inv, keep)
            for low, inv in zip(lows, invs)
        ]
        invs = [inv - paired_product(inv, m, keep) for inv, m in zip(invs, moved)]
        size *= 2
    return invs


def local_kernel(first_head, q_ref, k_ref, v_ref, ld_ref, wr_ref, ext_ref, pair_ref, state_ref):
    step = pl.program_id(0)
    n = CHUNK

    @pl.when(step == 0)
    def _():
        eye = jnp.where(iota2((DK, DK), 0) == iota2((DK, DK), 1), 1.0, 0.0)
        start = jnp.concatenate([eye, jnp.zeros((DK, DK), F32)], axis=1)
        for h in range(2):
            state_ref[h] = start

    row, col = iota2((n, 2 * n), 0), iota2((n, 2 * n), 1)
    is_first = col < n
    col = col % n
    strict, causal = row > col, row >= col
    tri = jnp.where(iota2((n, n), 0) >= iota2((n, n), 1), 1.0, 0.0).astype(BF)
    keep = (iota2((2 * n, 2 * n), 0) < n) == (iota2((2 * n, 2 * n), 1) < n)
    eye128 = iota2((DK, DK), 0) == iota2((DK, DK), 1)
    lows, reaches, details = [], [], []
    for c in range(PER_STEP):
        rows = slice(c * n, (c + 1) * n)
        logs = ld_ref[rows, :]
        one = logs.astype(BF)
        two, three = split2(logs - one.astype(F32))
        summed_all = dg(tri, one, NN) + (dg(tri, two, NN) + dg(tri, three, NN))
        lifted, downs, kept = [], [], []
        for h in range(2):
            lanes = slice(h * DK, (h + 1) * DK)
            queries = unit_rows(q_ref[rows, lanes].astype(F32))
            keyed = unit_rows(k_ref[rows, lanes].astype(F32))
            rate = wr_ref[rows, first_head + h : first_head + h + 1]
            summed = summed_all[:, lanes]
            middle = summed[n // 2 - 1 : n // 2, :]
            last = summed[n - 1 : n, :]
            rising = jnp.exp(summed - middle)
            downs.append(keyed * jnp.exp(middle - summed))
            lifted.append(jnp.concatenate([keyed * rising, queries * rising], axis=0))
            grown = jnp.exp(summed)
            entry = jnp.concatenate([keyed * grown, queries * grown], axis=0)
            to_end = keyed * jnp.exp(last - summed)
            decay = jnp.sum(jnp.where(eye128, jnp.exp(last), 0.0), axis=1, keepdims=True)
            kept.append((rate, entry, to_end, decay))
        down_h, down_l = split2(jnp.concatenate(downs, axis=0))
        scores = []
        for h in range(2):
            lh, ll = split2(lifted[h])
            scores.append(dot3_split(lh, ll, down_h, down_l, NT))
        rates = jnp.where(is_first, kept[0][0], kept[1][0])
        key_part = jnp.where(is_first, scores[0][:n], scores[1][:n])
        query_part = jnp.where(is_first, scores[0][n:], scores[1][n:])
        lows.append(jnp.where(strict, key_part * rates, 0.0))
        reaches.append(jnp.where(causal, query_part, 0.0))
        details.append(kept)
    invs = unit_lower_inverses(lows, keep)
    for c in range(PER_STEP):
        rows = slice(c * n, (c + 1) * n)
        states, targets, seen_out = [], [], []
        for h in range(2):
            rate, entry, to_end, decay = details[c][h]
            state = state_ref[h]
            seen = dot3(entry, state)
            values = v_ref[rows, h * DK : (h + 1) * DK].astype(F32)
            target = jnp.concatenate([-seen[:n, :DK], values - seen[:n, DK:]], axis=1)
            targets.append(target * rate)
            states.append(state)
            seen_out.append(seen[n:])
        ih, il = split2(invs[c])
        th, tl = split2(jnp.concatenate(targets, axis=0))
        fresh = dot3_split(two_blocks(ih, keep), two_blocks(il, keep), th, tl)
        fh, fl = split2(fresh)
        rh, rl = split2(reaches[c])
        spread = dot3_split(two_blocks(rh, keep), two_blocks(rl, keep), fh, fl)
        for h in range(2):
            rate, entry, to_end, decay = details[c][h]
            part = slice(h * n, (h + 1) * n)
            ext_ref[h, rows, :] = seen_out[h] + spread[part]
            eh, el = split2(to_end)
            state_ref[h] = states[h] * decay + (
                dg(eh, fh[part], TN) + (dg(eh, fl[part], TN) + dg(el, fh[part], TN))
            )

    @pl.when(step == pl.num_programs(0) - 1)
    def _():
        for h in range(2):
            state = state_ref[h]
            shifted = state[:, :DK] - jnp.where(eye128, 1.0, 0.0)
            pair_ref[h] = jnp.concatenate([shifted, state[:, DK:]], axis=1).astype(BF)


def local_chain(q, k, v, ld, wr, group):
    tokens = q.shape[0]
    heads = wr.shape[1]
    span = CHUNK * PER_STEP
    block = pl.BlockSpec((span, 2 * DK), lambda i: (i, group))

    def kernel(*refs):
        local_kernel(2 * group, *refs)

    return pl.pallas_call(
        kernel,
        grid=(tokens // span,),
        in_specs=[block, block, block, block, pl.BlockSpec((span, heads), lambda i: (i, 0))],
        out_specs=[
            pl.BlockSpec((2, span, 2 * DK), lambda i: (0, i, 0)),
            pl.BlockSpec((2, DK, 2 * DK), lambda i: (0, 0, 0)),
        ],
        out_shape=[
            jax.ShapeDtypeStruct((2, tokens, 2 * DK), F32),
            jax.ShapeDtypeStruct((2, DK, 2 * DK), BF),
        ],
        scratch_shapes=[pltpu.VMEM((2, DK, 2 * DK), F32)],
        interpret=INTERPRET,
        name="local_chain",
    )(q, k, v, ld, wr)


def prefix_kernel(place_ref, *refs):
    sources, (before_ref, total_ref, parts_ref) = refs[:-3], refs[-3:]
    count = parts_ref.shape[0]
    place = place_ref[0]
    for g in range(2):
        for i in range(count):
            source_ref = sources[g * count + i]
            parts_ref[i, g * 2 * DK : (g + 1) * 2 * DK, :] = source_ref[: 2 * DK, :]
    eye = jnp.where(iota2((DK, DK), 0) == iota2((DK, DK), 1), 1.0, 0.0)
    zero = jnp.zeros((DK, DK), F32)
    running = [jnp.concatenate([eye, zero], axis=1) for _ in range(4)]
    kept = list(running)
    for k in range(count):
        source = lax.rem(k - place + count, count)
        for h in range(4):
            part = parts_ref[source, h * DK : (h + 1) * DK, :]
            shift = jnp.concatenate([zero, part[:, DK:].astype(F32)], axis=1)
            running[h] = running[h] + (exact_left(part[:, :DK], running[h]) + shift)
            if k + 1 < count:
                kept[h] = jnp.where(place > k, running[h], kept[h])
    for h in range(4):
        before_ref[h] = kept[h]
        shifted = running[h][:, :DK] - eye
        total_ref[h] = jnp.concatenate([shifted, running[h][:, DK:]], axis=1).astype(BF)


def shard_prefix(place, parts):
    shape = (4, DK, 2 * DK)
    vm = pl.BlockSpec(memory_space=pltpu.VMEM)
    return pl.pallas_call(
        prefix_kernel,
        in_specs=[pl.BlockSpec(memory_space=pltpu.SMEM)] + [vm] * len(parts),
        out_specs=[vm, vm],
        out_shape=[jax.ShapeDtypeStruct(shape, F32), jax.ShapeDtypeStruct(shape, BF)],
        scratch_shapes=[pltpu.VMEM((len(parts) // 2, 4 * DK, 2 * DK), BF)],
        interpret=INTERPRET,
        name="shard_prefix",
    )(place, *parts)


def finish_kernel(place_ref, *refs):
    totals, (before_ref, first_ref, second_ref, out_ref) = refs[:-4], refs[-4:]
    place, core = place_ref[0], place_ref[1]
    lanes, rows = out_ref.shape[1], out_ref.shape[2]
    exts = (first_ref, second_ref)
    for h in range(4):
        state = jnp.zeros((DK, DK), F32)
        for i, total_ref in enumerate(totals):
            part = total_ref[h]
            moved = state + (exact_left(part[:, :DK], state) + part[:, DK:].astype(F32))
            state = jnp.where(place >= len(totals) - i, moved, state)
        before = before_ref[h]
        incoming = dot3(before[:, :DK], state) + before[:, DK:]
        ext = exts[h // 2][h % 2]
        head_out = ext[:, DK:] + dot3(ext[:, :DK], incoming)
        mean = jnp.mean(head_out * head_out, axis=-1, keepdims=True)
        normed = (head_out * lax.rsqrt(mean + 1e-06)).astype(BF)
        for i in range(2 * lanes):
            away = jnp.where(core == i % 2, 0, 1)
            out_ref[away, i // 2, :, h * DK : (h + 1) * DK] = normed[i * rows : (i + 1) * rows]


def finish_heads(place, totals, before, exts, lanes):
    tokens = exts[0].shape[1]
    vm = pl.BlockSpec(memory_space=pltpu.VMEM)
    return pl.pallas_call(
        finish_kernel,
        in_specs=[pl.BlockSpec(memory_space=pltpu.SMEM)] + [vm] * (len(totals) + 3),
        out_specs=vm,
        out_shape=jax.ShapeDtypeStruct((2, lanes, tokens // (2 * lanes), 4 * DK), BF),
        interpret=INTERPRET,
        name="finish_heads",
    )(place, *totals, before, *exts)


def turn(n, d):
    return [(i, (i + d) % n) for i in range(n)]


def exchange(x, dests):
    width = x.shape[1]
    return lax.all_to_all(
        x.reshape(dests, SLOTS, width), PLANE, split_axis=0, concat_axis=0, tiled=True
    ).reshape(dests * SLOTS, width)


def ring_gather(own, axis):
    n = lax.axis_size(axis)
    found = [None] * n
    found[0] = up = down = own
    for s in range(1, n // 2 + 1):
        up = lax.ppermute(up, axis, turn(n, 1))
        found[n - s] = up
        if s < n // 2:
            down = lax.ppermute(down, axis, turn(n, n - 1))
            found[s] = down
    return found


def ring_reduce(parts, axis):
    n = len(parts)
    half = n // 2
    up, down = parts[half], parts[half + 1]
    for s in range(half, 0, -1):
        up = lax.ppermute(up, axis, turn(n, 1)).astype(F32)
        if s > 1:
            up = (up + parts[s - 1].astype(F32)).astype(BF)
        if s > 1:
            down = lax.ppermute(down, axis, turn(n, n - 1)).astype(F32)
            if s > 2:
                down = (down + parts[n + 1 - s + 1].astype(F32)).astype(BF)
    return up + down + parts[0].astype(F32)


def routing_info(routes, route_gates):
    rows, picks = routes.shape
    high, low = split2(route_gates)
    pad = jnp.zeros((rows, picks), BF)
    info = jnp.concatenate([routes.astype(BF), high, low, pad], axis=1)
    info = info.reshape(rows * picks * 4 // (2 * DK), 2 * DK)
    return jnp.concatenate([info, jnp.zeros_like(info)], axis=0)


def routing_tables(info, picks, z, nz, dests, lane_count):
    count = info.shape[0]
    info = info.astype(F32)
    routes = info[:, :picks]
    gates = info[:, picks : 2 * picks] + info[:, 2 * picks : 3 * picks]
    dest = jnp.arange(dests, dtype=jnp.int32)
    expert_of = ((dest // lane_count) * nz + z) * lane_count + dest % lane_count
    hit = routes[:, :, None] == expert_of[None, None, :].astype(F32)
    member = jnp.any(hit, axis=1)
    gate = jnp.sum(jnp.where(hit, gates[:, :, None], 0.0), axis=1)
    earlier = (jnp.arange(count)[:, None] > jnp.arange(count)[None, :]).astype(BF)
    rank = jnp.dot(earlier, member.astype(BF), preferred_element_type=F32)
    rank = jnp.where(member, rank, -1.0)
    slot = jnp.arange(SLOTS, dtype=F32)
    chosen = (rank.T[:, None, :] == slot[None, :, None]).astype(BF).reshape(dests * SLOTS, count)
    weigh = jnp.where(rank[:, :, None] == slot[None, None, :], gate[:, :, None], 0.0)
    weigh = weigh.reshape(count, dests * SLOTS)
    weigh_hi = weigh.astype(BF)
    weigh_lo = (weigh - weigh_hi.astype(F32)).astype(BF)
    return chosen, weigh_hi, weigh_lo


def exchange(x, dests):
    width = x.shape[1]
    return lax.all_to_all(
        x.reshape(dests, SLOTS, width), PLANE, split_axis=0, concat_axis=0, tiled=True
    ).reshape(dests * SLOTS, width)


def per_device(
    residual, q, k, v, log_decay, write_rate, output_weight, routes, route_gates, up, down
):
    y, z = lax.axis_index(Y), lax.axis_index(Z)
    x, core = lax.axis_index(X), lax.axis_index(C)
    ny, nz = lax.axis_size(Y), lax.axis_size(Z)
    nx, nc = lax.axis_size(X), lax.axis_size(C)
    rows, width = residual.shape
    picks = routes.shape[1]
    dests, count = ny * nx * nc, nz * rows

    partner_weight = lax.ppermute(output_weight, C, turn(nc, 1))
    weights = jnp.concatenate([output_weight, partner_weight], axis=0)
    info = routing_info(routes, route_gates)
    exts, parts = [], []
    for group in range(2):
        ext, pair = local_chain(q, k, v, log_decay, write_rate, group)
        load = pair.reshape(2 * DK, 2 * DK)
        if group == 0:
            load = jnp.concatenate([load, info], axis=0)
        exts.append(ext)
        parts.append(ring_gather(load, Z))
    before, total = shard_prefix(z.reshape(1), parts[0] + parts[1])
    named = slice(2 * DK, 2 * DK + info.shape[0] // 2)
    shared = jnp.concatenate([part[named].reshape(rows, 4 * picks) for part in parts[0]], axis=0)
    tables = routing_tables(shared, picks, z, nz, dests, nx * nc)
    earlier = [lax.ppermute(total, Y, turn(ny, d)) for d in range(ny - 1, 0, -1)]
    earlier, tables = lax.optimization_barrier((earlier, tables))
    chosen, weigh_hi, weigh_lo = tables
    halves = finish_heads(jnp.stack([y, core]), earlier, before, exts, nx)

    mine = halves[0].reshape(nx * rows, -1)
    theirs = lax.ppermute(halves[1], C, turn(nc, 1)).reshape(nx * rows, -1)
    both = jnp.concatenate([mine, theirs], axis=1)
    cuts = (slice(0, CUT), slice(CUT, width))
    mixed, gathered = [], []
    for cols in cuts:
        partial = jnp.dot(both, weights[:, cols], preferred_element_type=F32)
        partial = partial.reshape(nx, rows, -1)
        attended = lax.dynamic_index_in_dim(partial, x, 0, keepdims=False)
        small = partial.astype(BF)
        for d in (2, 1, 3):
            sent = lax.dynamic_index_in_dim(small, (x + d) % nx, 0, keepdims=False)
            attended = attended + lax.ppermute(sent, X, turn(nx, d)).astype(F32)
        mixed.append((residual[:, cols].astype(F32) + attended).astype(BF))
        gathered.append(jnp.concatenate(ring_gather(mixed[-1], Z), axis=0))
    column = jnp.concatenate(gathered, axis=1).astype(F32)
    column = (
        column * lax.rsqrt(jnp.mean(column * column, axis=-1, keepdims=True) + 1e-06)
    ).astype(BF)
    outgoing = jnp.dot(chosen, column, preferred_element_type=F32).astype(BF)
    arrived = exchange(outgoing, dests)
    half = down.shape[1]
    gate_up = jnp.dot(arrived, up[0], preferred_element_type=F32)
    hidden = (jax.nn.silu(gate_up[:, :half]) * gate_up[:, half:]).astype(BF)
    results = jnp.dot(hidden, down[0], preferred_element_type=F32).astype(BF)
    returned = exchange(results, dests)
    outs = []
    for cols, base in zip(cuts, mixed):
        combined = (
            jnp.dot(weigh_hi, returned[:, cols], preferred_element_type=F32)
            + jnp.dot(weigh_lo, returned[:, cols], preferred_element_type=F32)
        ).astype(BF)
        combined = combined.reshape(nz, rows, -1)
        summed = ring_reduce([combined[r] for r in range(nz)], Z)
        outs.append((base.astype(F32) + summed).astype(BF))
    return jnp.concatenate(outs, axis=1)


def solution(mesh):
    finer = Mesh(mesh.devices.reshape(4, 8, 4, 2), (Y, Z, X, C))
    seq, lanes = (Y, Z), (X, C)
    in_specs = (
        P(ALL, None),
        P(seq, lanes),
        P(seq, lanes),
        P(seq, lanes),
        P(seq, lanes),
        P(seq, lanes),
        P(lanes, None),
        P(ALL, None),
        P(ALL, None),
        P(ALL, None, None),
        P(ALL, None, None),
    )
    return jax.shard_map(
        per_device, mesh=finer, in_specs=in_specs, out_specs=P(ALL, None), check_vma=False
    )
```

```python
import jax
import jax.numpy as jnp
from jax import lax
from jax.experimental import pallas as pl
from jax.experimental.pallas import tpu as pltpu
from jax.sharding import Mesh
from jax.sharding import PartitionSpec as P

CHUNK = 64
PER_STEP = 4
DK = 128
SLOTS = 32
CUT = 1024
Z, Y, X, C = "seq_1", "seq_0", "lane", "core"
ALL = (Y, Z, X, C)
PLANE = (Y, X, C)
BF = jnp.bfloat16
F32 = jnp.float32
INTERPRET = False


def split2(x):
    hi = x.astype(BF)
    return hi, (x - hi.astype(F32)).astype(BF)


def dg(a, b, dims):
    return lax.dot_general(a, b, (dims, ((), ())), preferred_element_type=F32)


NN = ((1,), (0,))
NT = ((1,), (1,))
TN = ((0,), (0,))


def dot3(a, b, dims=NN):
    ah, al = split2(a)
    bh, bl = split2(b)
    return dot3_split(ah, al, bh, bl, dims)


def dot3_split(ah, al, bh, bl, dims=NN):
    m = ah.shape[0]
    main = dg(jnp.concatenate([ah, al], axis=0), bh, dims)
    return main[:m] + (main[m:] + dg(ah, bl, dims))


def exact_left(a, b, dims=NN):
    bh, bl = split2(b)
    return dg(a, bh, dims) + dg(a, bl, dims)


def unit_rows(x):
    return x * lax.rsqrt(jnp.sum(x * x, axis=-1, keepdims=True) + 1e-06)


def iota2(shape, dim):
    return lax.broadcasted_iota(jnp.int32, shape, dim)


def two_blocks(x, keep):
    return jnp.where(keep, jnp.concatenate([x, x], axis=0), jnp.zeros((), x.dtype))


def paired_product(a, b, keep):
    ah, al = split2(a)
    bh, bl = split2(b)
    return dot3_split(ah, al, two_blocks(bh, keep), two_blocks(bl, keep))


def unit_lower_inverses(lows, keep):
    n = CHUNK
    row, col = iota2((n, 2 * n), 0), iota2((n, 2 * n), 1) % n
    eye = jnp.where(row == col, 1.0, 0.0)
    inner = [jnp.where(row // 8 == col // 8, low, 0.0) for low in lows]
    second = [paired_product(i, i, keep) for i in inner]
    invs = [eye - i for i in inner]
    fourth = [paired_product(s, s, keep) for s in second]
    invs = [inv + paired_product(inv, s, keep) for inv, s in zip(invs, second)]
    invs = [inv + paired_product(inv, f, keep) for inv, f in zip(invs, fourth)]
    size = 16
    while size <= n:
        half = size // 2
        between = (row // size == col // size) & (row // half != col // half)
        moved = [
            paired_product(jnp.where(between, low, 0.0), inv, keep)
            for low, inv in zip(lows, invs)
        ]
        invs = [inv - paired_product(inv, m, keep) for inv, m in zip(invs, moved)]
        size *= 2
    return invs


def local_kernel(first_head, resumed, final, q_ref, k_ref, v_ref, ld_ref, wr_ref, *refs):
    given_ref, ext_ref, pair_ref, state_ref = refs if resumed else (None, *refs)
    step = pl.program_id(0)
    n = CHUNK

    @pl.when(step == 0)
    def _():
        eye = jnp.where(iota2((DK, DK), 0) == iota2((DK, DK), 1), 1.0, 0.0)
        start = jnp.concatenate([eye, jnp.zeros((DK, DK), F32)], axis=1)
        for h in range(2):
            state_ref[h] = given_ref[h] if resumed else start

    row, col = iota2((n, 2 * n), 0), iota2((n, 2 * n), 1)
    is_first = col < n
    col = col % n
    strict, causal = row > col, row >= col
    tri = jnp.where(iota2((n, n), 0) >= iota2((n, n), 1), 1.0, 0.0).astype(BF)
    keep = (iota2((2 * n, 2 * n), 0) < n) == (iota2((2 * n, 2 * n), 1) < n)
    eye128 = iota2((DK, DK), 0) == iota2((DK, DK), 1)
    lows, reaches, details = [], [], []
    for c in range(PER_STEP):
        rows = slice(c * n, (c + 1) * n)
        logs = ld_ref[rows, :]
        one = logs.astype(BF)
        two, three = split2(logs - one.astype(F32))
        summed_all = dg(tri, one, NN) + (dg(tri, two, NN) + dg(tri, three, NN))
        lifted, downs, kept = [], [], []
        for h in range(2):
            lanes = slice(h * DK, (h + 1) * DK)
            queries = unit_rows(q_ref[rows, lanes].astype(F32))
            keyed = unit_rows(k_ref[rows, lanes].astype(F32))
            rate = wr_ref[rows, first_head + h : first_head + h + 1]
            summed = summed_all[:, lanes]
            middle = summed[n // 2 - 1 : n // 2, :]
            last = summed[n - 1 : n, :]
            rising = jnp.exp(summed - middle)
            downs.append(keyed * jnp.exp(middle - summed))
            lifted.append(jnp.concatenate([keyed * rising, queries * rising], axis=0))
            grown = jnp.exp(summed)
            entry = jnp.concatenate([keyed * grown, queries * grown], axis=0)
            to_end = keyed * jnp.exp(last - summed)
            decay = jnp.sum(jnp.where(eye128, jnp.exp(last), 0.0), axis=1, keepdims=True)
            kept.append((rate, entry, to_end, decay))
        down_h, down_l = split2(jnp.concatenate(downs, axis=0))
        scores = []
        for h in range(2):
            lh, ll = split2(lifted[h])
            scores.append(dot3_split(lh, ll, down_h, down_l, NT))
        rates = jnp.where(is_first, kept[0][0], kept[1][0])
        key_part = jnp.where(is_first, scores[0][:n], scores[1][:n])
        query_part = jnp.where(is_first, scores[0][n:], scores[1][n:])
        lows.append(jnp.where(strict, key_part * rates, 0.0))
        reaches.append(jnp.where(causal, query_part, 0.0))
        details.append(kept)
    invs = unit_lower_inverses(lows, keep)
    for c in range(PER_STEP):
        rows = slice(c * n, (c + 1) * n)
        states, targets, seen_out = [], [], []
        for h in range(2):
            rate, entry, to_end, decay = details[c][h]
            state = state_ref[h]
            seen = dot3(entry, state)
            values = v_ref[rows, h * DK : (h + 1) * DK].astype(F32)
            target = jnp.concatenate([-seen[:n, :DK], values - seen[:n, DK:]], axis=1)
            targets.append(target * rate)
            states.append(state)
            seen_out.append(seen[n:])
        ih, il = split2(invs[c])
        th, tl = split2(jnp.concatenate(targets, axis=0))
        fresh = dot3_split(two_blocks(ih, keep), two_blocks(il, keep), th, tl)
        fh, fl = split2(fresh)
        rh, rl = split2(reaches[c])
        spread = dot3_split(two_blocks(rh, keep), two_blocks(rl, keep), fh, fl)
        for h in range(2):
            rate, entry, to_end, decay = details[c][h]
            part = slice(h * n, (h + 1) * n)
            ext_ref[h, rows, :] = seen_out[h] + spread[part]
            eh, el = split2(to_end)
            state_ref[h] = states[h] * decay + (
                dg(eh, fh[part], TN) + (dg(eh, fl[part], TN) + dg(el, fh[part], TN))
            )

    @pl.when(step == pl.num_programs(0) - 1)
    def _():
        for h in range(2):
            state = state_ref[h]
            if final:
                shifted = state[:, :DK] - jnp.where(eye128, 1.0, 0.0)
                state = jnp.concatenate([shifted, state[:, DK:]], axis=1).astype(BF)
            pair_ref[h] = state


def local_chain(q, k, v, ld, wr, group, first=0, steps=None, given=None, final=True):
    heads = wr.shape[1]
    span = CHUNK * PER_STEP
    steps = q.shape[0] // span if steps is None else steps
    block = pl.BlockSpec((span, 2 * DK), lambda i: (i + first, group))
    whole = pl.BlockSpec((2, DK, 2 * DK), lambda i: (0, 0, 0))

    def kernel(*refs):
        local_kernel(2 * group, given is not None, final, *refs)

    rates = pl.BlockSpec((span, heads), lambda i: (i + first, 0))
    return pl.pallas_call(
        kernel,
        grid=(steps,),
        in_specs=[block, block, block, block, rates] + ([] if given is None else [whole]),
        out_specs=[pl.BlockSpec((2, span, 2 * DK), lambda i: (0, i, 0)), whole],
        out_shape=[
            jax.ShapeDtypeStruct((2, steps * span, 2 * DK), F32),
            jax.ShapeDtypeStruct((2, DK, 2 * DK), BF if final else F32),
        ],
        scratch_shapes=[pltpu.VMEM((2, DK, 2 * DK), F32)],
        interpret=INTERPRET,
        name="local_chain",
    )(q, k, v, ld, wr, *([] if given is None else [given]))


def prefix_kernel(place_ref, *refs):
    sources, (before_ref, total_ref, parts_ref) = refs[:-3], refs[-3:]
    count = parts_ref.shape[0]
    place = place_ref[0]
    for i, source_ref in enumerate(sources):
        parts_ref[i] = source_ref[: 2 * DK, :]
    eye = jnp.where(iota2((DK, DK), 0) == iota2((DK, DK), 1), 1.0, 0.0)
    zero = jnp.zeros((DK, DK), F32)
    running = [jnp.concatenate([eye, zero], axis=1) for _ in range(2)]
    kept = list(running)
    for k in range(count):
        source = lax.rem(k - place + count, count)
        for h in range(2):
            part = parts_ref[source, h * DK : (h + 1) * DK, :]
            shift = jnp.concatenate([zero, part[:, DK:].astype(F32)], axis=1)
            running[h] = running[h] + (exact_left(part[:, :DK], running[h]) + shift)
            if k + 1 < count:
                kept[h] = jnp.where(place > k, running[h], kept[h])
    for h in range(2):
        before_ref[h] = kept[h]
        shifted = running[h][:, :DK] - eye
        total_ref[h] = jnp.concatenate([shifted, running[h][:, DK:]], axis=1).astype(BF)


def shard_prefix(place, parts):
    shape = (2, DK, 2 * DK)
    vm = pl.BlockSpec(memory_space=pltpu.VMEM)
    return pl.pallas_call(
        prefix_kernel,
        in_specs=[pl.BlockSpec(memory_space=pltpu.SMEM)] + [vm] * len(parts),
        out_specs=[vm, vm],
        out_shape=[jax.ShapeDtypeStruct(shape, F32), jax.ShapeDtypeStruct(shape, BF)],
        scratch_shapes=[pltpu.VMEM((len(parts), 2 * DK, 2 * DK), BF)],
        interpret=INTERPRET,
        name="shard_prefix",
    )(place, *parts)


def finish_kernel(pieces, steps, place_ref, *refs):
    place, core = place_ref[0], place_ref[1]
    count = steps * 2 + 2
    totals = (refs[:steps], refs[steps : 2 * steps])
    befores = refs[2 * steps : count]
    ext_refs = refs[count:-2]
    mine_ref, theirs_ref = refs[-2:]
    rows = mine_ref.shape[1]
    for h in range(4):
        state = jnp.zeros((DK, DK), F32)
        for i, total_ref in enumerate(totals[h // 2]):
            part = total_ref[h % 2]
            moved = state + (exact_left(part[:, :DK], state) + part[:, DK:].astype(F32))
            state = jnp.where(place >= steps - i, moved, state)
        before = befores[h // 2][h % 2]
        incoming = dot3(before[:, :DK], state) + before[:, DK:]
        own = ext_refs[:1] if h < 2 else ext_refs[1:]
        lanes = slice(h * DK, (h + 1) * DK)
        block = 0
        for ext_ref in own:
            ext = ext_ref[h % 2]
            head_out = ext[:, DK:] + dot3(ext[:, :DK], incoming)
            mean = jnp.mean(head_out * head_out, axis=-1, keepdims=True)
            normed = (head_out * lax.rsqrt(mean + 1e-06)).astype(BF)
            for i in range(ext.shape[0] // (2 * rows)):
                even = normed[2 * i * rows : (2 * i + 1) * rows]
                odd = normed[(2 * i + 1) * rows : (2 * i + 2) * rows]
                mine_ref[block, :, lanes] = jnp.where(core == 0, even, odd)
                theirs_ref[block, :, lanes] = jnp.where(core == 0, odd, even)
                block += 1


def finish_heads(place, totals, befores, exts, lanes, rows):
    vm = pl.BlockSpec(memory_space=pltpu.VMEM)
    steps = len(totals[0])

    def kernel(*refs):
        finish_kernel(len(exts), steps, *refs)

    shape = jax.ShapeDtypeStruct((lanes, rows, 4 * DK), BF)
    operands = [*totals[0], *totals[1], *befores, *exts]
    return pl.pallas_call(
        kernel,
        in_specs=[pl.BlockSpec(memory_space=pltpu.SMEM)] + [vm] * len(operands),
        out_specs=[vm, vm],
        out_shape=[shape, shape],
        interpret=INTERPRET,
        name="finish_heads",
    )(place, *operands)


def turn(n, d):
    return [(i, (i + d) % n) for i in range(n)]


def exchange(x, dests):
    width = x.shape[1]
    return lax.all_to_all(
        x.reshape(dests, SLOTS, width), PLANE, split_axis=0, concat_axis=0, tiled=True
    ).reshape(dests * SLOTS, width)


def ring_begin(own, axis):
    n = lax.axis_size(axis)
    return [own] + [None] * (n - 1), own, own


def ring_step(ring, s, axis):
    found, up, down = ring
    n = len(found)
    up = lax.ppermute(up, axis, turn(n, 1))
    found[n - s] = up
    if s < n // 2:
        down = lax.ppermute(down, axis, turn(n, n - 1))
        found[s] = down
    return found, up, down


def ring_gather(own, axis):
    ring = ring_begin(own, axis)
    for s in range(1, lax.axis_size(axis) // 2 + 1):
        ring = ring_step(ring, s, axis)
    return ring[0]


def ring_reduce(parts, axis):
    n = len(parts)
    half = n // 2
    up, down = parts[half], parts[half + 1]
    for s in range(half, 0, -1):
        up = lax.ppermute(up, axis, turn(n, 1)).astype(F32)
        if s > 1:
            up = (up + parts[s - 1].astype(F32)).astype(BF)
        if s > 1:
            down = lax.ppermute(down, axis, turn(n, n - 1)).astype(F32)
            if s > 2:
                down = (down + parts[n + 1 - s + 1].astype(F32)).astype(BF)
    return up + down + parts[0].astype(F32)


def routing_info(routes, route_gates):
    rows, picks = routes.shape
    high, low = split2(route_gates)
    pad = jnp.zeros((rows, picks), BF)
    info = jnp.concatenate([routes.astype(BF), high, low, pad], axis=1)
    info = info.reshape(rows * picks * 4 // (2 * DK), 2 * DK)
    return jnp.concatenate([info, jnp.zeros_like(info)], axis=0)


def routing_tables(info, picks, z, nz, dests, lane_count):
    count = info.shape[0]
    info = info.astype(F32)
    routes = info[:, :picks]
    gates = info[:, picks : 2 * picks] + info[:, 2 * picks : 3 * picks]
    dest = jnp.arange(dests, dtype=jnp.int32)
    expert_of = ((dest // lane_count) * nz + z) * lane_count + dest % lane_count
    hit = routes[:, :, None] == expert_of[None, None, :].astype(F32)
    member = jnp.any(hit, axis=1)
    gate = jnp.sum(jnp.where(hit, gates[:, :, None], 0.0), axis=1)
    earlier = (jnp.arange(count)[:, None] > jnp.arange(count)[None, :]).astype(BF)
    rank = jnp.dot(earlier, member.astype(BF), preferred_element_type=F32)
    rank = jnp.where(member, rank, -1.0)
    slot = jnp.arange(SLOTS, dtype=F32)
    chosen = (rank.T[:, None, :] == slot[None, :, None]).astype(BF).reshape(dests * SLOTS, count)
    weigh = jnp.where(rank[:, :, None] == slot[None, None, :], gate[:, :, None], 0.0)
    weigh = weigh.reshape(count, dests * SLOTS)
    weigh_hi = weigh.astype(BF)
    weigh_lo = (weigh - weigh_hi.astype(F32)).astype(BF)
    return chosen, weigh_hi, weigh_lo


def exchange(x, dests):
    width = x.shape[1]
    return lax.all_to_all(
        x.reshape(dests, SLOTS, width), PLANE, split_axis=0, concat_axis=0, tiled=True
    ).reshape(dests * SLOTS, width)


def per_device(
    residual, q, k, v, log_decay, write_rate, output_weight, routes, route_gates, up, down
):
    y, z = lax.axis_index(Y), lax.axis_index(Z)
    x, core = lax.axis_index(X), lax.axis_index(C)
    ny, nz = lax.axis_size(Y), lax.axis_size(Z)
    nx, nc = lax.axis_size(X), lax.axis_size(C)
    rows, width = residual.shape
    picks = routes.shape[1]
    dests, count = ny * nx * nc, nz * rows

    partner_weight = lax.ppermute(output_weight, C, turn(nc, 1))
    info = routing_info(routes, route_gates)
    inputs = (q, k, v, log_decay, write_rate)
    per_call = q.shape[0] // (CHUNK * PER_STEP) // 2
    ext_a, pair_a = local_chain(*inputs, 0)
    load = jnp.concatenate([pair_a.reshape(2 * DK, 2 * DK), info], axis=0)
    ring = ring_step(ring_begin(load, Z), 1, Z)
    ext_b, state = local_chain(*inputs, 1, 0, per_call, None, False)
    found, up_a, down_a = ring
    up_a, down_a, state = lax.optimization_barrier((up_a, down_a, state))
    found[nz - 1], found[1] = up_a, down_a
    ring = ring_step((found, up_a, down_a), 2, Z)
    ext_c, pair_b = local_chain(*inputs, 1, per_call, per_call, state, True)
    for s in range(3, nz // 2 + 1):
        ring = ring_step(ring, s, Z)
    groups = (ring[0], ring_gather(pair_b.reshape(2 * DK, 2 * DK), Z))
    named = slice(2 * DK, 2 * DK + info.shape[0] // 2)
    shared = jnp.concatenate([part[named].reshape(rows, 4 * picks) for part in groups[0]], axis=0)
    tables = routing_tables(shared, picks, z, nz, dests, nx * nc)
    befores, earlier = [], []
    for parts in groups:
        before, total = shard_prefix(z.reshape(1), parts)
        befores.append(before)
        earlier.append([lax.ppermute(total, Y, turn(ny, d)) for d in range(ny - 1, 0, -1)])
    earlier, tables = lax.optimization_barrier((earlier, tables))
    chosen, weigh_hi, weigh_lo = tables
    mine, theirs = finish_heads(
        jnp.stack([y, core]), earlier, befores, (ext_a, ext_b, ext_c), nx, rows
    )
    theirs = lax.ppermute(theirs, C, turn(nc, 1)).reshape(nx * rows, -1)
    mine = mine.reshape(nx * rows, -1)
    cuts = (slice(0, CUT), slice(CUT, width))
    mixed, gathered = [], []
    for cols in cuts:
        partial = jnp.dot(mine, output_weight[:, cols], preferred_element_type=F32)
        partial = partial + jnp.dot(
            theirs, partner_weight[:, cols], preferred_element_type=F32
        )
        partial = partial.reshape(nx, rows, -1)
        attended = lax.dynamic_index_in_dim(partial, x, 0, keepdims=False)
        small = partial.astype(BF)
        for d in (2, 1, 3):
            sent = lax.dynamic_index_in_dim(small, (x + d) % nx, 0, keepdims=False)
            attended = attended + lax.ppermute(sent, X, turn(nx, d)).astype(F32)
        mixed.append((residual[:, cols].astype(F32) + attended).astype(BF))
        gathered.append(jnp.concatenate(ring_gather(mixed[-1], Z), axis=0))
    column = jnp.concatenate(gathered, axis=1).astype(F32)
    column = (
        column * lax.rsqrt(jnp.mean(column * column, axis=-1, keepdims=True) + 1e-06)
    ).astype(BF)
    outgoing = jnp.dot(chosen, column, preferred_element_type=F32).astype(BF)
    arrived = exchange(outgoing, dests)
    half = down.shape[1]
    gate_up = jnp.dot(arrived, up[0], preferred_element_type=F32)
    hidden = (jax.nn.silu(gate_up[:, :half]) * gate_up[:, half:]).astype(BF)
    results = jnp.dot(hidden, down[0], preferred_element_type=F32).astype(BF)
    returned = exchange(results, dests)
    outs = []
    for cols, base in zip(cuts, mixed):
        combined = (
            jnp.dot(weigh_hi, returned[:, cols], preferred_element_type=F32)
            + jnp.dot(weigh_lo, returned[:, cols], preferred_element_type=F32)
        ).astype(BF)
        combined = combined.reshape(nz, rows, -1)
        summed = ring_reduce([combined[r] for r in range(nz)], Z)
        outs.append((base.astype(F32) + summed).astype(BF))
    return jnp.concatenate(outs, axis=1)


def solution(mesh):
    finer = Mesh(mesh.devices.reshape(4, 8, 4, 2), (Y, Z, X, C))
    seq, lanes = (Y, Z), (X, C)
    in_specs = (
        P(ALL, None),
        P(seq, lanes),
        P(seq, lanes),
        P(seq, lanes),
        P(seq, lanes),
        P(seq, lanes),
        P(lanes, None),
        P(ALL, None),
        P(ALL, None),
        P(ALL, None, None),
        P(ALL, None, None),
    )
    return jax.shard_map(
        per_device, mesh=finer, in_specs=in_specs, out_specs=P(ALL, None), check_vma=False
    )
```

```python
import jax
import jax.numpy as jnp
from jax import lax
from jax.experimental import pallas as pl
from jax.experimental.pallas import tpu as pltpu
from jax.sharding import Mesh
from jax.sharding import PartitionSpec as P

CHUNK = 64
PER_STEP = 4
DK = 128
SLOTS = 32
CUT = 1024
Z, Y, X, C = "seq_1", "seq_0", "lane", "core"
ALL = (Y, Z, X, C)
PLANE = (Y, X, C)
BF = jnp.bfloat16
F32 = jnp.float32
INTERPRET = False


def split2(x):
    hi = x.astype(BF)
    return hi, (x - hi.astype(F32)).astype(BF)


def dg(a, b, dims):
    return lax.dot_general(a, b, (dims, ((), ())), preferred_element_type=F32)


NN = ((1,), (0,))
NT = ((1,), (1,))
TN = ((0,), (0,))


def dot3(a, b, dims=NN):
    ah, al = split2(a)
    bh, bl = split2(b)
    return dot3_split(ah, al, bh, bl, dims)


def dot3_split(ah, al, bh, bl, dims=NN):
    m = ah.shape[0]
    main = dg(jnp.concatenate([ah, al], axis=0), bh, dims)
    return main[:m] + (main[m:] + dg(ah, bl, dims))


def exact_left(a, b, dims=NN):
    bh, bl = split2(b)
    return dg(a, bh, dims) + dg(a, bl, dims)


def unit_rows(x):
    return x * lax.rsqrt(jnp.sum(x * x, axis=-1, keepdims=True) + 1e-06)


def iota2(shape, dim):
    return lax.broadcasted_iota(jnp.int32, shape, dim)


def two_blocks(x, keep):
    return jnp.where(keep, jnp.concatenate([x, x], axis=0), jnp.zeros((), x.dtype))


def paired_product(a, b, keep):
    ah, al = split2(a)
    bh, bl = split2(b)
    return dot3_split(ah, al, two_blocks(bh, keep), two_blocks(bl, keep))


def unit_lower_inverses(lows, keep):
    n = CHUNK
    row, col = iota2((n, 2 * n), 0), iota2((n, 2 * n), 1) % n
    eye = jnp.where(row == col, 1.0, 0.0)
    inner = [jnp.where(row // 8 == col // 8, low, 0.0) for low in lows]
    second = [paired_product(i, i, keep) for i in inner]
    invs = [eye - i for i in inner]
    fourth = [paired_product(s, s, keep) for s in second]
    invs = [inv + paired_product(inv, s, keep) for inv, s in zip(invs, second)]
    invs = [inv + paired_product(inv, f, keep) for inv, f in zip(invs, fourth)]
    size = 16
    while size <= n:
        half = size // 2
        between = (row // size == col // size) & (row // half != col // half)
        moved = [
            paired_product(jnp.where(between, low, 0.0), inv, keep)
            for low, inv in zip(lows, invs)
        ]
        invs = [inv - paired_product(inv, m, keep) for inv, m in zip(invs, moved)]
        size *= 2
    return invs


def local_kernel(first_head, q_ref, k_ref, v_ref, ld_ref, wr_ref, ext_ref, pair_ref, state_ref):
    step = pl.program_id(0)
    n = CHUNK

    @pl.when(step == 0)
    def _():
        eye = jnp.where(iota2((DK, DK), 0) == iota2((DK, DK), 1), 1.0, 0.0)
        start = jnp.concatenate([eye, jnp.zeros((DK, DK), F32)], axis=1)
        for h in range(2):
            state_ref[h] = start

    row, col = iota2((n, 2 * n), 0), iota2((n, 2 * n), 1)
    is_first = col < n
    col = col % n
    strict, causal = row > col, row >= col
    tri = jnp.where(iota2((n, n), 0) >= iota2((n, n), 1), 1.0, 0.0).astype(BF)
    keep = (iota2((2 * n, 2 * n), 0) < n) == (iota2((2 * n, 2 * n), 1) < n)
    eye128 = iota2((DK, DK), 0) == iota2((DK, DK), 1)
    eye64 = iota2((n, n), 0) == iota2((n, n), 1)
    lows, reaches, details = [], [], []
    for c in range(PER_STEP):
        rows = slice(c * n, (c + 1) * n)
        logs = ld_ref[rows, :]
        one = logs.astype(BF)
        two, three = split2(logs - one.astype(F32))
        summed_all = dg(tri, one, NN) + (dg(tri, two, NN) + dg(tri, three, NN))
        lifted, downs, kept = [], [], []
        for h in range(2):
            lanes = slice(h * DK, (h + 1) * DK)
            queries = unit_rows(q_ref[rows, lanes].astype(F32))
            keyed = unit_rows(k_ref[rows, lanes].astype(F32))
            rate_row = wr_ref[first_head + h : first_head + h + 1, rows]
            rate = jnp.sum(jnp.where(eye64, rate_row, 0.0), axis=1, keepdims=True)
            summed = summed_all[:, lanes]
            middle = summed[n // 2 - 1 : n // 2, :]
            last = summed[n - 1 : n, :]
            rising = jnp.exp(summed - middle)
            downs.append(keyed * jnp.exp(middle - summed))
            lifted.append(jnp.concatenate([keyed * rising, queries * rising], axis=0))
            grown = jnp.exp(summed)
            entry = jnp.concatenate([keyed * grown, queries * grown], axis=0)
            to_end = keyed * jnp.exp(last - summed)
            decay = jnp.sum(jnp.where(eye128, jnp.exp(last), 0.0), axis=1, keepdims=True)
            kept.append((rate, entry, to_end, decay))
        down_h, down_l = split2(jnp.concatenate(downs, axis=0))
        scores = []
        for h in range(2):
            lh, ll = split2(lifted[h])
            scores.append(dot3_split(lh, ll, down_h, down_l, NT))
        rates = jnp.where(is_first, kept[0][0], kept[1][0])
        key_part = jnp.where(is_first, scores[0][:n], scores[1][:n])
        query_part = jnp.where(is_first, scores[0][n:], scores[1][n:])
        lows.append(jnp.where(strict, key_part * rates, 0.0))
        reaches.append(jnp.where(causal, query_part, 0.0))
        details.append(kept)
    invs = unit_lower_inverses(lows, keep)
    for c in range(PER_STEP):
        rows = slice(c * n, (c + 1) * n)
        states, targets, seen_out = [], [], []
        for h in range(2):
            rate, entry, to_end, decay = details[c][h]
            state = state_ref[h]
            seen = dot3(entry, state)
            values = v_ref[rows, h * DK : (h + 1) * DK].astype(F32)
            target = jnp.concatenate([-seen[:n, :DK], values - seen[:n, DK:]], axis=1)
            targets.append(target * rate)
            states.append(state)
            seen_out.append(seen[n:])
        ih, il = split2(invs[c])
        th, tl = split2(jnp.concatenate(targets, axis=0))
        fresh = dot3_split(two_blocks(ih, keep), two_blocks(il, keep), th, tl)
        fh, fl = split2(fresh)
        rh, rl = split2(reaches[c])
        spread = dot3_split(two_blocks(rh, keep), two_blocks(rl, keep), fh, fl)
        for h in range(2):
            rate, entry, to_end, decay = details[c][h]
            part = slice(h * n, (h + 1) * n)
            ext_ref[h, rows, :] = seen_out[h] + spread[part]
            eh, el = split2(to_end)
            state_ref[h] = states[h] * decay + (
                dg(eh, fh[part], TN) + (dg(eh, fl[part], TN) + dg(el, fh[part], TN))
            )

    @pl.when(step == pl.num_programs(0) - 1)
    def _():
        for h in range(2):
            state = state_ref[h]
            shifted = state[:, :DK] - jnp.where(eye128, 1.0, 0.0)
            pair_ref[h] = jnp.concatenate([shifted, state[:, DK:]], axis=1).astype(BF)


def local_chain(q, k, v, ld, wr, group):
    tokens = q.shape[0]
    heads = wr.shape[0]
    span = CHUNK * PER_STEP
    block = pl.BlockSpec((span, 2 * DK), lambda i: (i, group))

    def kernel(*refs):
        local_kernel(2 * group, *refs)

    return pl.pallas_call(
        kernel,
        grid=(tokens // span,),
        in_specs=[block, block, block, block, pl.BlockSpec((heads, span), lambda i: (0, i))],
        out_specs=[
            pl.BlockSpec((2, span, 2 * DK), lambda i: (0, i, 0)),
            pl.BlockSpec((2, DK, 2 * DK), lambda i: (0, 0, 0)),
        ],
        out_shape=[
            jax.ShapeDtypeStruct((2, tokens, 2 * DK), F32),
            jax.ShapeDtypeStruct((2, DK, 2 * DK), BF),
        ],
        scratch_shapes=[pltpu.VMEM((2, DK, 2 * DK), F32)],
        interpret=INTERPRET,
        name="local_chain",
    )(q, k, v, ld, wr)


def prefix_kernel(place_ref, *refs):
    sources, (before_ref, total_ref, parts_ref) = refs[:-3], refs[-3:]
    count = parts_ref.shape[0]
    place = place_ref[0]
    for g in range(2):
        for i in range(count):
            source_ref = sources[g * count + i]
            parts_ref[i, g * 2 * DK : (g + 1) * 2 * DK, :] = source_ref[: 2 * DK, :]
    eye = jnp.where(iota2((DK, DK), 0) == iota2((DK, DK), 1), 1.0, 0.0)
    zero = jnp.zeros((DK, DK), F32)
    running = [jnp.concatenate([eye, zero], axis=1) for _ in range(4)]
    kept = list(running)
    for k in range(count):
        source = lax.rem(k - place + count, count)
        for h in range(4):
            part = parts_ref[source, h * DK : (h + 1) * DK, :]
            shift = jnp.concatenate([zero, part[:, DK:].astype(F32)], axis=1)
            running[h] = running[h] + (exact_left(part[:, :DK], running[h]) + shift)
            if k + 1 < count:
                kept[h] = jnp.where(place > k, running[h], kept[h])
    for h in range(4):
        before_ref[h] = kept[h]
        shifted = running[h][:, :DK] - eye
        total_ref[h] = jnp.concatenate([shifted, running[h][:, DK:]], axis=1).astype(BF)


def shard_prefix(place, parts):
    shape = (4, DK, 2 * DK)
    vm = pl.BlockSpec(memory_space=pltpu.VMEM)
    return pl.pallas_call(
        prefix_kernel,
        in_specs=[pl.BlockSpec(memory_space=pltpu.SMEM)] + [vm] * len(parts),
        out_specs=[vm, vm],
        out_shape=[jax.ShapeDtypeStruct(shape, F32), jax.ShapeDtypeStruct(shape, BF)],
        scratch_shapes=[pltpu.VMEM((len(parts) // 2, 4 * DK, 2 * DK), BF)],
        interpret=INTERPRET,
        name="shard_prefix",
    )(place, *parts)


def finish_kernel(place_ref, *refs):
    totals = refs[:-5]
    before_ref, first_ref, second_ref, mine_ref, theirs_ref = refs[-5:]
    place, core = place_ref[0], place_ref[1]
    rows = mine_ref.shape[1]
    for h in range(4):
        state = jnp.zeros((DK, DK), F32)
        for i, total_ref in enumerate(totals):
            part = total_ref[h]
            moved = state + (exact_left(part[:, :DK], state) + part[:, DK:].astype(F32))
            state = jnp.where(place >= len(totals) - i, moved, state)
        before = before_ref[h]
        incoming = dot3(before[:, :DK], state) + before[:, DK:]
        lanes = slice(h * DK, (h + 1) * DK)
        ext = (first_ref, second_ref)[h // 2][h % 2]
        head_out = ext[:, DK:] + dot3(ext[:, :DK], incoming)
        mean = jnp.mean(head_out * head_out, axis=-1, keepdims=True)
        normed = (head_out * lax.rsqrt(mean + 1e-06)).astype(BF)
        for i in range(mine_ref.shape[0]):
            even = normed[2 * i * rows : (2 * i + 1) * rows]
            odd = normed[(2 * i + 1) * rows : (2 * i + 2) * rows]
            mine_ref[i, :, lanes] = jnp.where(core == 0, even, odd)
            theirs_ref[i, :, lanes] = jnp.where(core == 0, odd, even)


def finish_heads(place, totals, before, exts, lanes, rows):
    vm = pl.BlockSpec(memory_space=pltpu.VMEM)
    shape = jax.ShapeDtypeStruct((lanes, rows, 4 * DK), BF)
    operands = [*totals, before, *exts]
    return pl.pallas_call(
        finish_kernel,
        in_specs=[pl.BlockSpec(memory_space=pltpu.SMEM)] + [vm] * len(operands),
        out_specs=[vm, vm],
        out_shape=[shape, shape],
        interpret=INTERPRET,
        name="finish_heads",
    )(place, *operands)


def turn(n, d):
    return [(i, (i + d) % n) for i in range(n)]


def exchange(x, dests):
    width = x.shape[1]
    return lax.all_to_all(
        x.reshape(dests, SLOTS, width), PLANE, split_axis=0, concat_axis=0, tiled=True
    ).reshape(dests * SLOTS, width)


def ring_gather(own, axis):
    n = lax.axis_size(axis)
    found = [None] * n
    found[0] = up = down = own
    for s in range(1, n // 2 + 1):
        up = lax.ppermute(up, axis, turn(n, 1))
        found[n - s] = up
        if s < n // 2:
            down = lax.ppermute(down, axis, turn(n, n - 1))
            found[s] = down
    return found


def ring_reduce(parts, axis):
    n = len(parts)
    half = n // 2
    up, down = parts[half], parts[half + 1]
    for s in range(half, 0, -1):
        up = lax.ppermute(up, axis, turn(n, 1)).astype(F32)
        if s > 1:
            up = (up + parts[s - 1].astype(F32)).astype(BF)
        if s > 1:
            down = lax.ppermute(down, axis, turn(n, n - 1)).astype(F32)
            if s > 2:
                down = (down + parts[n + 1 - s + 1].astype(F32)).astype(BF)
    return up + down + parts[0].astype(F32)


def routing_info(routes, route_gates):
    rows, picks = routes.shape
    high, low = split2(route_gates)
    pad = jnp.zeros((rows, picks), BF)
    info = jnp.concatenate([routes.astype(BF), high, low, pad], axis=1)
    info = info.reshape(rows * picks * 4 // (2 * DK), 2 * DK)
    return jnp.concatenate([info, jnp.zeros_like(info)], axis=0)


def routing_tables(info, picks, z, nz, dests, lane_count):
    count = info.shape[0]
    info = info.astype(F32)
    routes = info[:, :picks]
    gates = info[:, picks : 2 * picks] + info[:, 2 * picks : 3 * picks]
    dest = jnp.arange(dests, dtype=jnp.int32)
    expert_of = ((dest // lane_count) * nz + z) * lane_count + dest % lane_count
    hit = routes[:, :, None] == expert_of[None, None, :].astype(F32)
    member = jnp.any(hit, axis=1)
    gate = jnp.sum(jnp.where(hit, gates[:, :, None], 0.0), axis=1)
    earlier = (jnp.arange(count)[:, None] > jnp.arange(count)[None, :]).astype(BF)
    rank = jnp.dot(earlier, member.astype(BF), preferred_element_type=F32)
    rank = jnp.where(member, rank, -1.0)
    slot = jnp.arange(SLOTS, dtype=F32)
    chosen = (rank.T[:, None, :] == slot[None, :, None]).astype(BF).reshape(dests * SLOTS, count)
    weigh = jnp.where(rank[:, :, None] == slot[None, None, :], gate[:, :, None], 0.0)
    weigh = weigh.reshape(count, dests * SLOTS)
    weigh_hi = weigh.astype(BF)
    weigh_lo = (weigh - weigh_hi.astype(F32)).astype(BF)
    return chosen, weigh_hi, weigh_lo


def exchange(x, dests):
    width = x.shape[1]
    return lax.all_to_all(
        x.reshape(dests, SLOTS, width), PLANE, split_axis=0, concat_axis=0, tiled=True
    ).reshape(dests * SLOTS, width)


def per_device(
    residual, q, k, v, log_decay, write_rate, output_weight, routes, route_gates, up, down
):
    y, z = lax.axis_index(Y), lax.axis_index(Z)
    x, core = lax.axis_index(X), lax.axis_index(C)
    ny, nz = lax.axis_size(Y), lax.axis_size(Z)
    nx, nc = lax.axis_size(X), lax.axis_size(C)
    rows, width = residual.shape
    picks = routes.shape[1]
    dests, count = ny * nx * nc, nz * rows

    partner_weight = lax.ppermute(output_weight, C, turn(nc, 1))
    info = routing_info(routes, route_gates)
    rates = write_rate.T
    exts, parts = [], []
    for group in range(2):
        ext, pair = local_chain(q, k, v, log_decay, rates, group)
        load = pair.reshape(2 * DK, 2 * DK)
        if group == 0:
            load = jnp.concatenate([load, info], axis=0)
        exts.append(ext)
        parts.append(ring_gather(load, Z))
    before, total = shard_prefix(z.reshape(1), parts[0] + parts[1])
    named = slice(2 * DK, 2 * DK + info.shape[0] // 2)
    shared = jnp.concatenate([part[named].reshape(rows, 4 * picks) for part in parts[0]], axis=0)
    tables = routing_tables(shared, picks, z, nz, dests, nx * nc)
    earlier = [lax.ppermute(total, Y, turn(ny, d)) for d in range(ny - 1, 0, -1)]
    earlier, tables = lax.optimization_barrier((earlier, tables))
    chosen, weigh_hi, weigh_lo = tables
    mine, theirs = finish_heads(jnp.stack([y, core]), earlier, before, exts, nx, rows)
    theirs = lax.ppermute(theirs, C, turn(nc, 1)).reshape(nx * rows, -1)
    mine = mine.reshape(nx * rows, -1)
    cuts = (slice(0, CUT), slice(CUT, width))
    mixed, gathered = [], []
    for cols in cuts:
        partial = jnp.dot(mine, output_weight[:, cols], preferred_element_type=F32)
        partial = partial + jnp.dot(
            theirs, partner_weight[:, cols], preferred_element_type=F32
        )
        partial = partial.reshape(nx, rows, -1)
        attended = lax.dynamic_index_in_dim(partial, x, 0, keepdims=False)
        small = partial.astype(BF)
        for d in (2, 1, 3):
            sent = lax.dynamic_index_in_dim(small, (x + d) % nx, 0, keepdims=False)
            attended = attended + lax.ppermute(sent, X, turn(nx, d)).astype(F32)
        mixed.append((residual[:, cols].astype(F32) + attended).astype(BF))
        gathered.append(jnp.concatenate(ring_gather(mixed[-1], Z), axis=0))
    column = jnp.concatenate(gathered, axis=1).astype(F32)
    column = (
        column * lax.rsqrt(jnp.mean(column * column, axis=-1, keepdims=True) + 1e-06)
    ).astype(BF)
    outgoing = jnp.dot(chosen, column, preferred_element_type=F32).astype(BF)
    arrived = exchange(outgoing, dests)
    half = down.shape[1]
    gate_up = jnp.dot(arrived, up[0], preferred_element_type=F32)
    hidden = (jax.nn.silu(gate_up[:, :half]) * gate_up[:, half:]).astype(BF)
    results = jnp.dot(hidden, down[0], preferred_element_type=F32).astype(BF)
    returned = exchange(results, dests)
    outs = []
    for cols, base in zip(cuts, mixed):
        combined = (
            jnp.dot(weigh_hi, returned[:, cols], preferred_element_type=F32)
            + jnp.dot(weigh_lo, returned[:, cols], preferred_element_type=F32)
        ).astype(BF)
        combined = combined.reshape(nz, rows, -1)
        summed = ring_reduce([combined[r] for r in range(nz)], Z)
        outs.append((base.astype(F32) + summed).astype(BF))
    return jnp.concatenate(outs, axis=1)


def solution(mesh):
    finer = Mesh(mesh.devices.reshape(4, 8, 4, 2), (Y, Z, X, C))
    seq, lanes = (Y, Z), (X, C)
    in_specs = (
        P(ALL, None),
        P(seq, lanes),
        P(seq, lanes),
        P(seq, lanes),
        P(seq, lanes),
        P(seq, lanes),
        P(lanes, None),
        P(ALL, None),
        P(ALL, None),
        P(ALL, None, None),
        P(ALL, None, None),
    )
    return jax.shard_map(
        per_device, mesh=finer, in_specs=in_specs, out_specs=P(ALL, None), check_vma=False
    )
```

```python
import jax
import jax.numpy as jnp
from jax import lax
from jax.experimental import pallas as pl
from jax.experimental.pallas import tpu as pltpu
from jax.sharding import Mesh
from jax.sharding import PartitionSpec as P

CHUNK = 64
PER_STEP = 8
DK = 128
SLOTS = 32
CUT = 1024
Z, Y, X, C = "seq_1", "seq_0", "lane", "core"
ALL = (Y, Z, X, C)
PLANE = (Y, X, C)
BF = jnp.bfloat16
F32 = jnp.float32
INTERPRET = False


def split2(x):
    hi = x.astype(BF)
    return hi, (x - hi.astype(F32)).astype(BF)


def dg(a, b, dims):
    return lax.dot_general(a, b, (dims, ((), ())), preferred_element_type=F32)


NN = ((1,), (0,))
NT = ((1,), (1,))
TN = ((0,), (0,))


def dot3(a, b, dims=NN):
    ah, al = split2(a)
    bh, bl = split2(b)
    return dot3_split(ah, al, bh, bl, dims)


def dot3_split(ah, al, bh, bl, dims=NN):
    m = ah.shape[0]
    main = dg(jnp.concatenate([ah, al], axis=0), bh, dims)
    return main[:m] + (main[m:] + dg(ah, bl, dims))


def exact_left(a, b, dims=NN):
    bh, bl = split2(b)
    return dg(a, bh, dims) + dg(a, bl, dims)


def unit_rows(x):
    return x * lax.rsqrt(jnp.sum(x * x, axis=-1, keepdims=True) + 1e-06)


def iota2(shape, dim):
    return lax.broadcasted_iota(jnp.int32, shape, dim)


def two_blocks(x, keep):
    return jnp.where(keep, jnp.concatenate([x, x], axis=0), jnp.zeros((), x.dtype))


def paired_product(a, b, keep):
    ah, al = split2(a)
    bh, bl = split2(b)
    return dot3_split(ah, al, two_blocks(bh, keep), two_blocks(bl, keep))


def unit_lower_inverses(lows, keep):
    n = CHUNK
    row, col = iota2((n, 2 * n), 0), iota2((n, 2 * n), 1) % n
    eye = jnp.where(row == col, 1.0, 0.0)
    inner = [jnp.where(row // 8 == col // 8, low, 0.0) for low in lows]
    second = [paired_product(i, i, keep) for i in inner]
    invs = [eye - i for i in inner]
    fourth = [paired_product(s, s, keep) for s in second]
    invs = [inv + paired_product(inv, s, keep) for inv, s in zip(invs, second)]
    invs = [inv + paired_product(inv, f, keep) for inv, f in zip(invs, fourth)]
    size = 16
    while size <= n:
        half = size // 2
        between = (row // size == col // size) & (row // half != col // half)
        moved = [
            paired_product(jnp.where(between, low, 0.0), inv, keep)
            for low, inv in zip(lows, invs)
        ]
        invs = [inv - paired_product(inv, m, keep) for inv, m in zip(invs, moved)]
        size *= 2
    return invs


def local_kernel(first_head, q_ref, k_ref, v_ref, ld_ref, wr_ref, ext_ref, pair_ref, state_ref):
    step = pl.program_id(0)
    n = CHUNK

    @pl.when(step == 0)
    def _():
        eye = jnp.where(iota2((DK, DK), 0) == iota2((DK, DK), 1), 1.0, 0.0)
        start = jnp.concatenate([eye, jnp.zeros((DK, DK), F32)], axis=1)
        for h in range(2):
            state_ref[h] = start

    row, col = iota2((n, 2 * n), 0), iota2((n, 2 * n), 1)
    is_first = col < n
    col = col % n
    strict, causal = row > col, row >= col
    tri = jnp.where(iota2((n, n), 0) >= iota2((n, n), 1), 1.0, 0.0).astype(BF)
    keep = (iota2((2 * n, 2 * n), 0) < n) == (iota2((2 * n, 2 * n), 1) < n)
    eye128 = iota2((DK, DK), 0) == iota2((DK, DK), 1)
    eye64 = iota2((n, n), 0) == iota2((n, n), 1)
    lows, reaches, details = [], [], []
    for c in range(PER_STEP):
        rows = slice(c * n, (c + 1) * n)
        logs = ld_ref[rows, :]
        one = logs.astype(BF)
        two, three = split2(logs - one.astype(F32))
        summed_all = dg(tri, one, NN) + (dg(tri, two, NN) + dg(tri, three, NN))
        lifted, downs, kept = [], [], []
        for h in range(2):
            lanes = slice(h * DK, (h + 1) * DK)
            queries = unit_rows(q_ref[rows, lanes].astype(F32))
            keyed = unit_rows(k_ref[rows, lanes].astype(F32))
            rate_row = wr_ref[first_head + h : first_head + h + 1, rows]
            rate = jnp.sum(jnp.where(eye64, rate_row, 0.0), axis=1, keepdims=True)
            summed = summed_all[:, lanes]
            middle = summed[n // 2 - 1 : n // 2, :]
            last = summed[n - 1 : n, :]
            rising = jnp.exp(summed - middle)
            downs.append(keyed * jnp.exp(middle - summed))
            lifted.append(jnp.concatenate([keyed * rising, queries * rising], axis=0))
            grown = jnp.exp(summed)
            entry = jnp.concatenate([keyed * grown, queries * grown], axis=0)
            to_end = keyed * jnp.exp(last - summed)
            decay = jnp.sum(jnp.where(eye128, jnp.exp(last), 0.0), axis=1, keepdims=True)
            kept.append((rate, entry, to_end, decay))
        down_h, down_l = split2(jnp.concatenate(downs, axis=0))
        scores = []
        for h in range(2):
            lh, ll = split2(lifted[h])
            scores.append(dot3_split(lh, ll, down_h, down_l, NT))
        rates = jnp.where(is_first, kept[0][0], kept[1][0])
        key_part = jnp.where(is_first, scores[0][:n], scores[1][:n])
        query_part = jnp.where(is_first, scores[0][n:], scores[1][n:])
        lows.append(jnp.where(strict, key_part * rates, 0.0))
        reaches.append(jnp.where(causal, query_part, 0.0))
        details.append(kept)
    invs = unit_lower_inverses(lows, keep)
    for c in range(PER_STEP):
        rows = slice(c * n, (c + 1) * n)
        states, targets, seen_out = [], [], []
        for h in range(2):
            rate, entry, to_end, decay = details[c][h]
            state = state_ref[h]
            seen = dot3(entry, state)
            values = v_ref[rows, h * DK : (h + 1) * DK].astype(F32)
            target = jnp.concatenate([-seen[:n, :DK], values - seen[:n, DK:]], axis=1)
            targets.append(target * rate)
            states.append(state)
            seen_out.append(seen[n:])
        ih, il = split2(invs[c])
        th, tl = split2(jnp.concatenate(targets, axis=0))
        fresh = dot3_split(two_blocks(ih, keep), two_blocks(il, keep), th, tl)
        fh, fl = split2(fresh)
        rh, rl = split2(reaches[c])
        spread = dot3_split(two_blocks(rh, keep), two_blocks(rl, keep), fh, fl)
        for h in range(2):
            rate, entry, to_end, decay = details[c][h]
            part = slice(h * n, (h + 1) * n)
            ext_ref[h, rows, :] = seen_out[h] + spread[part]
            eh, el = split2(to_end)
            state_ref[h] = states[h] * decay + (
                dg(eh, fh[part], TN) + (dg(eh, fl[part], TN) + dg(el, fh[part], TN))
            )

    @pl.when(step == pl.num_programs(0) - 1)
    def _():
        for h in range(2):
            state = state_ref[h]
            shifted = state[:, :DK] - jnp.where(eye128, 1.0, 0.0)
            pair_ref[h] = jnp.concatenate([shifted, state[:, DK:]], axis=1).astype(BF)


def local_chain(q, k, v, ld, wr, group):
    tokens = q.shape[0]
    heads = wr.shape[0]
    span = CHUNK * PER_STEP
    block = pl.BlockSpec((span, 2 * DK), lambda i: (i, group))

    def kernel(*refs):
        local_kernel(2 * group, *refs)

    return pl.pallas_call(
        kernel,
        grid=(tokens // span,),
        in_specs=[block, block, block, block, pl.BlockSpec((heads, span), lambda i: (0, i))],
        out_specs=[
            pl.BlockSpec((2, span, 2 * DK), lambda i: (0, i, 0)),
            pl.BlockSpec((2, DK, 2 * DK), lambda i: (0, 0, 0)),
        ],
        out_shape=[
            jax.ShapeDtypeStruct((2, tokens, 2 * DK), F32),
            jax.ShapeDtypeStruct((2, DK, 2 * DK), BF),
        ],
        scratch_shapes=[pltpu.VMEM((2, DK, 2 * DK), F32)],
        interpret=INTERPRET,
        name="local_chain",
    )(q, k, v, ld, wr)


def prefix_kernel(place_ref, *refs):
    sources, (before_ref, total_ref, parts_ref) = refs[:-3], refs[-3:]
    count = parts_ref.shape[0]
    place = place_ref[0]
    for g in range(2):
        for i in range(count):
            source_ref = sources[g * count + i]
            parts_ref[i, g * 2 * DK : (g + 1) * 2 * DK, :] = source_ref[: 2 * DK, :]
    eye = jnp.where(iota2((DK, DK), 0) == iota2((DK, DK), 1), 1.0, 0.0)
    zero = jnp.zeros((DK, DK), F32)
    running = [jnp.concatenate([eye, zero], axis=1) for _ in range(4)]
    kept = list(running)
    for k in range(count):
        source = lax.rem(k - place + count, count)
        for h in range(4):
            part = parts_ref[source, h * DK : (h + 1) * DK, :]
            shift = jnp.concatenate([zero, part[:, DK:].astype(F32)], axis=1)
            running[h] = running[h] + (exact_left(part[:, :DK], running[h]) + shift)
            if k + 1 < count:
                kept[h] = jnp.where(place > k, running[h], kept[h])
    for h in range(4):
        before_ref[h] = kept[h]
        shifted = running[h][:, :DK] - eye
        total_ref[h] = jnp.concatenate([shifted, running[h][:, DK:]], axis=1).astype(BF)


def shard_prefix(place, parts):
    shape = (4, DK, 2 * DK)
    vm = pl.BlockSpec(memory_space=pltpu.VMEM)
    return pl.pallas_call(
        prefix_kernel,
        in_specs=[pl.BlockSpec(memory_space=pltpu.SMEM)] + [vm] * len(parts),
        out_specs=[vm, vm],
        out_shape=[jax.ShapeDtypeStruct(shape, F32), jax.ShapeDtypeStruct(shape, BF)],
        scratch_shapes=[pltpu.VMEM((len(parts) // 2, 4 * DK, 2 * DK), BF)],
        interpret=INTERPRET,
        name="shard_prefix",
    )(place, *parts)


def finish_kernel(place_ref, *refs):
    totals = refs[:-5]
    before_ref, first_ref, second_ref, mine_ref, theirs_ref = refs[-5:]
    place, core = place_ref[0], place_ref[1]
    rows = mine_ref.shape[1]
    for h in range(4):
        state = jnp.zeros((DK, DK), F32)
        for i, total_ref in enumerate(totals):
            part = total_ref[h]
            moved = state + (exact_left(part[:, :DK], state) + part[:, DK:].astype(F32))
            state = jnp.where(place >= len(totals) - i, moved, state)
        before = before_ref[h]
        incoming = dot3(before[:, :DK], state) + before[:, DK:]
        lanes = slice(h * DK, (h + 1) * DK)
        ext = (first_ref, second_ref)[h // 2][h % 2]
        head_out = ext[:, DK:] + dot3(ext[:, :DK], incoming)
        mean = jnp.mean(head_out * head_out, axis=-1, keepdims=True)
        normed = (head_out * lax.rsqrt(mean + 1e-06)).astype(BF)
        for i in range(mine_ref.shape[0]):
            even = normed[2 * i * rows : (2 * i + 1) * rows]
            odd = normed[(2 * i + 1) * rows : (2 * i + 2) * rows]
            mine_ref[i, :, lanes] = jnp.where(core == 0, even, odd)
            theirs_ref[i, :, lanes] = jnp.where(core == 0, odd, even)


def finish_heads(place, totals, before, exts, lanes, rows):
    vm = pl.BlockSpec(memory_space=pltpu.VMEM)
    shape = jax.ShapeDtypeStruct((lanes, rows, 4 * DK), BF)
    operands = [*totals, before, *exts]
    return pl.pallas_call(
        finish_kernel,
        in_specs=[pl.BlockSpec(memory_space=pltpu.SMEM)] + [vm] * len(operands),
        out_specs=[vm, vm],
        out_shape=[shape, shape],
        interpret=INTERPRET,
        name="finish_heads",
    )(place, *operands)


def turn(n, d):
    return [(i, (i + d) % n) for i in range(n)]


def exchange(x, dests):
    width = x.shape[1]
    return lax.all_to_all(
        x.reshape(dests, SLOTS, width), PLANE, split_axis=0, concat_axis=0, tiled=True
    ).reshape(dests * SLOTS, width)


def ring_gather(own, axis):
    n = lax.axis_size(axis)
    found = [None] * n
    found[0] = up = down = own
    for s in range(1, n // 2 + 1):
        up = lax.ppermute(up, axis, turn(n, 1))
        found[n - s] = up
        if s < n // 2:
            down = lax.ppermute(down, axis, turn(n, n - 1))
            found[s] = down
    return found


def ring_reduce(parts, axis):
    n = len(parts)
    half = n // 2
    up, down = parts[half], parts[half + 1]
    for s in range(half, 0, -1):
        up = lax.ppermute(up, axis, turn(n, 1)).astype(F32)
        if s > 1:
            up = (up + parts[s - 1].astype(F32)).astype(BF)
        if s > 1:
            down = lax.ppermute(down, axis, turn(n, n - 1)).astype(F32)
            if s > 2:
                down = (down + parts[n + 1 - s + 1].astype(F32)).astype(BF)
    return up + down + parts[0].astype(F32)


def routing_info(routes, route_gates):
    rows, picks = routes.shape
    high, low = split2(route_gates)
    pad = jnp.zeros((rows, picks), BF)
    info = jnp.concatenate([routes.astype(BF), high, low, pad], axis=1)
    info = info.reshape(rows * picks * 4 // (2 * DK), 2 * DK)
    return jnp.concatenate([info, jnp.zeros_like(info)], axis=0)


def routing_tables(info, picks, z, nz, dests, lane_count):
    count = info.shape[0]
    info = info.astype(F32)
    routes = info[:, :picks]
    gates = info[:, picks : 2 * picks] + info[:, 2 * picks : 3 * picks]
    dest = jnp.arange(dests, dtype=jnp.int32)
    expert_of = ((dest // lane_count) * nz + z) * lane_count + dest % lane_count
    hit = routes[:, :, None] == expert_of[None, None, :].astype(F32)
    member = jnp.any(hit, axis=1)
    gate = jnp.sum(jnp.where(hit, gates[:, :, None], 0.0), axis=1)
    earlier = (jnp.arange(count)[:, None] > jnp.arange(count)[None, :]).astype(BF)
    rank = jnp.dot(earlier, member.astype(BF), preferred_element_type=F32)
    rank = jnp.where(member, rank, -1.0)
    slot = jnp.arange(SLOTS, dtype=F32)
    chosen = (rank.T[:, None, :] == slot[None, :, None]).astype(BF).reshape(dests * SLOTS, count)
    weigh = jnp.where(rank[:, :, None] == slot[None, None, :], gate[:, :, None], 0.0)
    weigh = weigh.reshape(count, dests * SLOTS)
    weigh_hi = weigh.astype(BF)
    weigh_lo = (weigh - weigh_hi.astype(F32)).astype(BF)
    return chosen, weigh_hi, weigh_lo


def exchange(x, dests):
    width = x.shape[1]
    return lax.all_to_all(
        x.reshape(dests, SLOTS, width), PLANE, split_axis=0, concat_axis=0, tiled=True
    ).reshape(dests * SLOTS, width)


def per_device(
    residual, q, k, v, log_decay, write_rate, output_weight, routes, route_gates, up, down
):
    y, z = lax.axis_index(Y), lax.axis_index(Z)
    x, core = lax.axis_index(X), lax.axis_index(C)
    ny, nz = lax.axis_size(Y), lax.axis_size(Z)
    nx, nc = lax.axis_size(X), lax.axis_size(C)
    rows, width = residual.shape
    picks = routes.shape[1]
    dests, count = ny * nx * nc, nz * rows

    partner_weight = lax.ppermute(output_weight, C, turn(nc, 1))
    info = routing_info(routes, route_gates)
    rates = write_rate.T
    exts, parts = [], []
    for group in range(2):
        ext, pair = local_chain(q, k, v, log_decay, rates, group)
        load = pair.reshape(2 * DK, 2 * DK)
        if group == 0:
            load = jnp.concatenate([load, info], axis=0)
        exts.append(ext)
        parts.append(ring_gather(load, Z))
    before, total = shard_prefix(z.reshape(1), parts[0] + parts[1])
    named = slice(2 * DK, 2 * DK + info.shape[0] // 2)
    shared = jnp.concatenate([part[named].reshape(rows, 4 * picks) for part in parts[0]], axis=0)
    tables = routing_tables(shared, picks, z, nz, dests, nx * nc)
    earlier = [lax.ppermute(total, Y, turn(ny, d)) for d in range(ny - 1, 0, -1)]
    earlier, tables = lax.optimization_barrier((earlier, tables))
    chosen, weigh_hi, weigh_lo = tables
    mine, theirs = finish_heads(jnp.stack([y, core]), earlier, before, exts, nx, rows)
    theirs = lax.ppermute(theirs, C, turn(nc, 1)).reshape(nx * rows, -1)
    mine = mine.reshape(nx * rows, -1)
    cuts = (slice(0, CUT), slice(CUT, width))
    mixed, gathered = [], []
    for cols in cuts:
        partial = jnp.dot(mine, output_weight[:, cols], preferred_element_type=F32)
        partial = partial + jnp.dot(
            theirs, partner_weight[:, cols], preferred_element_type=F32
        )
        partial = partial.reshape(nx, rows, -1)
        attended = lax.dynamic_index_in_dim(partial, x, 0, keepdims=False)
        small = partial.astype(BF)
        for d in (2, 1, 3):
            sent = lax.dynamic_index_in_dim(small, (x + d) % nx, 0, keepdims=False)
            attended = attended + lax.ppermute(sent, X, turn(nx, d)).astype(F32)
        mixed.append((residual[:, cols].astype(F32) + attended).astype(BF))
        gathered.append(jnp.concatenate(ring_gather(mixed[-1], Z), axis=0))
    column = jnp.concatenate(gathered, axis=1).astype(F32)
    column = (
        column * lax.rsqrt(jnp.mean(column * column, axis=-1, keepdims=True) + 1e-06)
    ).astype(BF)
    outgoing = jnp.dot(chosen, column, preferred_element_type=F32).astype(BF)
    arrived = exchange(outgoing, dests)
    half = down.shape[1]
    gate_up = jnp.dot(arrived, up[0], preferred_element_type=F32)
    hidden = (jax.nn.silu(gate_up[:, :half]) * gate_up[:, half:]).astype(BF)
    results = jnp.dot(hidden, down[0], preferred_element_type=F32).astype(BF)
    returned = exchange(results, dests)
    outs = []
    for cols, base in zip(cuts, mixed):
        combined = (
            jnp.dot(weigh_hi, returned[:, cols], preferred_element_type=F32)
            + jnp.dot(weigh_lo, returned[:, cols], preferred_element_type=F32)
        ).astype(BF)
        combined = combined.reshape(nz, rows, -1)
        summed = ring_reduce([combined[r] for r in range(nz)], Z)
        outs.append((base.astype(F32) + summed).astype(BF))
    return jnp.concatenate(outs, axis=1)


def solution(mesh):
    finer = Mesh(mesh.devices.reshape(4, 8, 4, 2), (Y, Z, X, C))
    seq, lanes = (Y, Z), (X, C)
    in_specs = (
        P(ALL, None),
        P(seq, lanes),
        P(seq, lanes),
        P(seq, lanes),
        P(seq, lanes),
        P(seq, lanes),
        P(lanes, None),
        P(ALL, None),
        P(ALL, None),
        P(ALL, None, None),
        P(ALL, None, None),
    )
    return jax.shard_map(
        per_device, mesh=finer, in_specs=in_specs, out_specs=P(ALL, None), check_vma=False
    )
```
